1024 devices in a mesh: ctx: 64 (over y_lo, x, core), tp: 16 (over y_hi, z).
Axes of the slice: x: 8, y: 8 (y_hi: 2, y_lo: 4; y = y_hi * 4 + y_lo), z: 8, core: 2. Of those that a mesh axis runs over, the one named last changes fastest.
Arguments:
- out_grad: bfloat16 [16384, 8192], P(('ctx', 'tp')), may hold values from -6 to 6
- saved_input: bfloat16 [16384, 8192], P(('ctx', 'tp')), may hold values from -6 to 6
- explicit_filter_weights: float32 [128, 8192], P(None, 'tp'), may hold values from -0.5 to 0.5
- gate_taps: float32 [3, 8192], P(None, 'tp'), may hold values from -3.5 to 3.5
- value_featurizer_weights: float32 [3, 8192], P(None, 'tp'), may hold values from -3.5 to 3.5
Outputs:
- input_grad: bfloat16 [16384, 8192], P('ctx', 'tp')
- explicit_filter_gradient: float32 [128, 8192], P(None, 'tp')
- gate_grad: float32 [3, 8192], P(None, 'tp')
- value_grad: float32 [3, 8192], P(None, 'tp')
The draws below stay inside these ranges and needn't reach their ends.
All inputs are finite; a program needn't handle non-finite values.
Results may differ from the reference program's by a relative error of at most 0.004.
Values may be sent and summed in bfloat16 or wider, within the bound.
A program may use at most 32 MiB of HBM per device.

```python
import jax
import jax.numpy as jnp
from jax import lax

D = 8192
FILTER_LENGTH = 128
FK = 3
TOKENS = 16384


def level_of(own_key, dims, shards, least, largest):
    level = 1.0
    for position, shards_of in shards:
        heights = jax.random.uniform(jax.random.fold_in(jax.random.fold_in(own_key, 6), position), (shards_of,), jnp.float32, least / len(shards), largest / len(shards))
        level = level * jnp.repeat(jnp.exp(heights), dims[position] // shards_of).reshape((-1,) + (1,) * (len(dims) - 1 - position))
    return level


def gaussian(key, extent, deviation, bound, pieces=(), kind=jnp.bfloat16):
    result = jax.random.normal(key, extent, jnp.float32) * deviation
    if len(pieces) > 0:
        result = level_of(key, extent, pieces, -0.22, 0.18) * result
    return jnp.clip(result, min=-bound, max=bound).astype(kind)


def setup_inputs(seed: int = 0) -> dict:
    arg_keys = jax.random.split(jax.random.key(seed), 6)
    out_grad = gaussian(arg_keys[0], (TOKENS, D), 1.0, 6.0, ((0, 1024),))
    saved_input = gaussian(arg_keys[1], (TOKENS, D), 1.0, 6.0, ((0, 1024),))
    explicit_filter_weights = gaussian(arg_keys[2], (FILTER_LENGTH, D), FILTER_LENGTH ** -0.5, 0.5, ((1, 16),), jnp.float32)
    gate_taps = gaussian(arg_keys[3], (FK, D), FK ** -0.5, 3.5, ((1, 16),), jnp.float32)
    value_featurizer_weights = gaussian(arg_keys[4], (FK, D), FK ** -0.5, 3.5, ((1, 16),), jnp.float32)
    return {"out_grad": out_grad, "saved_input": saved_input, "explicit_filter_weights": explicit_filter_weights, "gate_taps": gate_taps, "value_featurizer_weights": value_featurizer_weights}


def causal_mixing(padded, taps, count):
    filter_extent = taps.shape[0]
    total = taps[0] * padded[filter_extent - 1:filter_extent - 1 + count]
    for j in range(1, filter_extent):
        total = total + taps[j] * padded[filter_extent - 1 - j:filter_extent - 1 - j + count]
    return total


def anticausal(padded, taps, count):
    total = taps[0] * padded[0:count]
    for j in range(1, taps.shape[0]):
        total = total + taps[j] * padded[j:j + count]
    return total


def delayed_input(left, right, filter_extent, base):
    count = left.shape[0]
    return jnp.stack([jnp.sum(left * right[base - j:base - j + count], axis=0) for j in range(filter_extent)])


def compose(value_featurizer_weights, explicit_filter_weights):
    short = value_featurizer_weights.shape[0]
    filter_extent = explicit_filter_weights.shape[0]
    total = jnp.zeros((filter_extent + short - 1, explicit_filter_weights.shape[1]), jnp.float32)
    for i in range(short):
        total = total.at[i:i + filter_extent].add(value_featurizer_weights[i] * explicit_filter_weights)
    return total


def channel_block(args):
    out_grad, saved_input, explicit_filter_weights, gate_taps, value_featurizer_weights = args
    sequence_length = out_grad.shape[0]
    width = out_grad.shape[1]
    reach = FILTER_LENGTH + FK - 2
    extended_input = jnp.concatenate([jnp.zeros((reach, width), jnp.float32), saved_input.astype(jnp.float32)])
    extended_value = causal_mixing(extended_input, value_featurizer_weights, sequence_length + FILTER_LENGTH - 1)
    qext = causal_mixing(extended_input, gate_taps, sequence_length + FILTER_LENGTH - 1)
    gate = qext[FILTER_LENGTH - 1:]
    pext = causal_mixing(extended_input, explicit_filter_weights, sequence_length + FK - 1)
    mixed_signal = causal_mixing(extended_value, explicit_filter_weights, sequence_length)
    grad_f = out_grad.astype(jnp.float32)
    grad_q = grad_f * mixed_signal
    mixed_signal_gradient = grad_f * gate
    gradient_scale = jnp.float32(TOKENS ** -0.5)
    explicit_filter_gradient = delayed_input(mixed_signal_gradient, extended_value, FILTER_LENGTH, FILTER_LENGTH - 1) * gradient_scale
    gate_grad = delayed_input(grad_q, extended_input, FK, reach) * gradient_scale
    value_grad = delayed_input(mixed_signal_gradient, pext, FK, FK - 1) * gradient_scale
    combined = compose(value_featurizer_weights, explicit_filter_weights)
    zpad = jnp.concatenate([mixed_signal_gradient, jnp.zeros((reach, width), jnp.float32)])
    qpad = jnp.concatenate([grad_q, jnp.zeros((FK - 1, width), jnp.float32)])
    input_grad = anticausal(zpad, combined, sequence_length) + anticausal(qpad, gate_taps, sequence_length)
    return input_grad.astype(jnp.bfloat16), explicit_filter_gradient, gate_grad, value_grad


def reference(out_grad, saved_input, explicit_filter_weights, gate_taps, value_featurizer_weights):
    block = 512 if D % 512 == 0 else D
    count = D // block

    def split_cols(array):
        return array.reshape(array.shape[0], count, block).transpose(1, 0, 2)

    def join_cols(array):
        return array.transpose(1, 0, 2).reshape(array.shape[1], D)

    results = lax.map(channel_block, (split_cols(out_grad), split_cols(saved_input), split_cols(explicit_filter_weights), split_cols(gate_taps), split_cols(value_featurizer_weights)))
    return join_cols(results[0]), join_cols(results[1]), join_cols(results[2]), join_cols(results[3])
```

```python
import functools
import math

import jax
import jax.numpy as jnp
import ml_dtypes
import numpy as np
from jax import lax
from jax.experimental import pallas as pl
from jax.experimental.pallas import tpu as pltpu
from jax.sharding import PartitionSpec as P

MESH = pl.DeviceIdType.MESH
F32 = jnp.float32
BF16 = jnp.bfloat16
EXTRA = 8


def two_parts(matrix):
    high = matrix.astype(ml_dtypes.bfloat16)
    low = (matrix - high.astype(np.float64)).astype(ml_dtypes.bfloat16)
    return high, low


def transforms(length):
    odd = 2 * np.arange(length // 2)[:, None] + 1
    steps = (odd * np.arange(length)[None, :]) % (2 * length)
    angle = np.pi * steps / length
    forward = np.concatenate([np.cos(angle), -np.sin(angle)])
    inverse = forward.T * (2.0 / length)
    return two_parts(forward) + two_parts(inverse)


def split(x):
    high = x.astype(BF16)
    return high, (x - high.astype(F32)).astype(BF16)


def dot3(ah, al, xh, xl):
    def dot(a, b):
        return jnp.dot(a, b, preferred_element_type=F32)

    return dot(ah, xh) + dot(ah, xl) + dot(al, xh)


def kernel(
    sizes,
    og, si, h_hbm, gt_ref, w_ref, fh_hbm, fl_hbm, ih_hbm, il_hbm,
    ig_out, efg_out, gate_out, value_out,
    ubuf, gbuf, hb, fh, fl, ih, il,
    hs, vs, ds, uf, qb, zb, xh, xl, w1b, dqb, igb, head, head_in,
    part, part_in, ext, rs, xr, yr, ag, ext_in,
    a2a_send, a2a_recv, halo_send, halo_recv, head_send, head_recv,
    const_sem, one_send, one_recv,
):
    nctx, ntp, xs, ys, taps, scale = sizes
    rows, width = og.shape[0], og.shape[1] // ntp
    tokens = rows * ntp
    chans = width // 2
    halo = ubuf.shape[1] - tokens
    length = tokens + taps
    half_len = length // 2
    slice_rows = taps // xs
    ctx, tp = lax.axis_index("ctx"), lax.axis_index("tp")
    core = lax.rem(ctx, 2)
    x = lax.rem(ctx // 2, xs)
    ylo = ctx // (2 * xs)
    row16 = lax.rem(ctx, 2 * xs)

    def remote(src, dst, send, recv, to_ctx, to_tp):
        return pltpu.make_async_remote_copy(
            src_ref=src, dst_ref=dst, send_sem=send, recv_sem=recv,
            device_id=(to_ctx, to_tp), device_id_type=MESH,
        )

    def finish(ref, sem):
        pltpu.make_async_copy(ref, ref, sem).wait()

    def offset(k):
        half = (1 - core) if k == 0 else core
        return pl.multiple_of(half * chans, chans)

    def tp_peer(i):
        return lax.rem(tp + i, ntp)

    def row_peer(i):
        return ylo * (2 * xs) + lax.rem(row16 + i, 2 * xs)

    def x_peer(i):
        return lax.rem(x + i, xs)

    def x_ctx(other):
        return (ylo * xs + other) * 2 + core

    def y_ctx(i):
        return (lax.rem(ylo + i, ys) * xs + x) * 2 + core

    barrier = pltpu.get_barrier_semaphore()

    def greet(to_ctx, to_tp):
        pl.semaphore_signal(barrier, inc=1, device_id=(to_ctx, to_tp), device_id_type=MESH)

    def loop(count, body):
        def step(i, carry):
            body(i)
            return carry

        lax.fori_loop(1, count, step, 0)

    loop(ntp, lambda i: greet(ctx, tp_peer(i)))
    loop(2 * xs, lambda i: greet(row_peer(i), tp))
    loop(ys, lambda i: greet(y_ctx(i), tp))

    @pl.when(ctx > 0)
    def _():
        greet(ctx - 1, tp)

    @pl.when(ctx < nctx - 1)
    def _():
        greet(ctx + 1, tp)

    constants = [
        pltpu.make_async_copy(src, dst, const_sem.at[i])
        for i, (src, dst) in enumerate(
            [(fh_hbm, fh), (fl_hbm, fl), (ih_hbm, ih), (il_hbm, il)]
            + [(h_hbm.at[:, pl.ds(offset(k), chans)], hb.at[k]) for k in range(2)]
        )
    ]
    for copy in constants:
        copy.start()

    @pl.when(ctx == 0)
    def _():
        ubuf[:, 0:halo, :] = jnp.zeros((2, halo, chans), BF16)

    @pl.when(ctx == nctx - 1)
    def _():
        head_in[...] = jnp.zeros(head_in.shape, BF16)

    greeted = ntp - 1 + 2 * xs - 1 + ys - 1
    greeted = greeted + jnp.where(ctx > 0, 1, 0) + jnp.where(ctx < nctx - 1, 1, 0)
    pl.semaphore_wait(barrier, greeted)

    def exchange(src, dst, base, k, sem):
        def columns(who):
            return src.at[:, pl.ds(pl.multiple_of(who * width + offset(k), chans), chans)]

        place = dst.at[k, pl.ds(pl.multiple_of(base + tp * rows, 16), rows), :]
        loop(
            ntp,
            lambda i: remote(
                columns(tp_peer(i)), place, a2a_send.at[sem], a2a_recv.at[sem], ctx, tp_peer(i)
            ).start(),
        )
        pltpu.make_async_copy(columns(tp), place, a2a_recv.at[sem]).start()

    exchange(si, ubuf, halo, 0, 0)
    exchange(si, ubuf, halo, 1, 1)
    exchange(og, gbuf, 0, 0, 2)
    exchange(og, gbuf, 0, 1, 3)

    for copy in constants:
        copy.wait()
    for k in range(2):
        th, tl = split(hb[k])
        hs[k] = dot3(fh[:, 0:taps], fl[:, 0:taps], th, tl)
    w1b[:, 0:16, :] = jnp.zeros((2, 16, chans), F32)
    w1b[:, 16 + length : 32 + length, :] = jnp.zeros((2, 16, chans), F32)
    dqb[:, 0:16, :] = jnp.zeros((2, 16, chans), F32)
    dqb[:, 16 + tokens : 32 + tokens, :] = jnp.zeros((2, 16, chans), F32)

    def taps_of(ref, k):
        block = ref[:, pl.ds(offset(k), chans)]
        return [block[i : i + 1] for i in range(3)]

    def halo_copy(k):
        return remote(
            ubuf.at[k, pl.ds(tokens, halo), :], ubuf.at[1 - k, pl.ds(0, halo), :],
            halo_send.at[k], halo_recv.at[1 - k], ctx + 1, tp,
        )

    for k in range(2):
        finish(ubuf.at[k, pl.ds(halo, tokens), :], a2a_recv.at[k])

        @pl.when(ctx < nctx - 1)
        def _(k=k):
            halo_copy(k).start()

    def spectrum_product(a, a_k, b, b_k, sign):
        for r in range(0, half_len, 32):
            ar, ai = a[a_k, r : r + 32], a[a_k, half_len + r : half_len + r + 32]
            br, bi = b[b_k, r : r + 32], b[b_k, half_len + r : half_len + r + 32]
            if sign > 0:
                re, im = ar * br - ai * bi, ar * bi + ai * br
            else:
                re, im = ar * br + ai * bi, ar * bi - ai * br
            xh[r : r + 32], xl[r : r + 32] = split(re)
            xh[half_len + r : half_len + r + 32], xl[half_len + r : half_len + r + 32] = split(im)

    def delayed(k, r, count):
        first = halo - taps + r
        return [uf[k, first - i : first - i + count] for i in range(3)]

    for k in range(2):

        @pl.when(ctx > 0)
        def _(k=k):
            finish(ubuf.at[k, pl.ds(0, halo), :], halo_recv.at[k])

        for r in range(0, halo + tokens, 16):
            uf[k, r : r + 16] = ubuf[k, r : r + 16].astype(F32)
        wv, wg = taps_of(w_ref, k), taps_of(gt_ref, k)
        for r in range(0, length, 32):
            u = delayed(k, r, 32)
            v = wv[0] * u[0] + wv[1] * u[1] + wv[2] * u[2]
            xh[r : r + 32], xl[r : r + 32] = split(v)
            if r >= taps:
                qb[k, r - taps : r - taps + 32] = wg[0] * u[0] + wg[1] * u[1] + wg[2] * u[2]
        vs[k] = dot3(fh[...], fl[...], xh[...], xl[...])
        spectrum_product(hs, k, vs, k, 1)
        zb[k] = dot3(ih[taps:, :], il[taps:, :], xh[...], xl[...])

    def fold(values):
        return jnp.sum(values.reshape(values.shape[0] // 8, 8, chans), axis=0)

    def input_gradient(k):
        wv, wg = taps_of(w_ref, k), taps_of(gt_ref, k)
        for r in range(0, halo + tokens, 16):
            a = [w1b[k, r + i : r + i + 16] for i in range(3)]
            total = wv[0] * a[0] + wv[1] * a[1] + wv[2] * a[2]
            first = r - halo
            if first >= -16:
                d = [dqb[k, 16 + first + i : 32 + first + i] for i in range(3)]
                total = total + wg[0] * d[0] + wg[1] * d[1] + wg[2] * d[2]
            if first < 0:
                head[k, r : r + 16] = total.astype(BF16)
            else:
                igb[k, first : first + 16] = total

        @pl.when(ctx > 0)
        def _():
            remote(
                head.at[k], head_in.at[1 - k], head_send.at[k], head_recv.at[1 - k], ctx - 1, tp
            ).start()

    partner = ctx + 1 - 2 * core

    for k in range(2):
        finish(gbuf.at[k], a2a_recv.at[2 + k])
        gate_sums = [jnp.zeros((8, chans), F32) for _ in range(3)]
        for r in range(0, tokens, 32):
            g = gbuf[k, r : r + 32].astype(F32)
            xh[taps + r : taps + r + 32], xl[taps + r : taps + r + 32] = split(
                g * qb[k, r : r + 32]
            )
            dq = g * zb[k, r : r + 32]
            dqb[k, 16 + r : 48 + r] = dq
            u = delayed(k, taps + r, 32)
            gate_sums = [s + fold(dq * d) for s, d in zip(gate_sums, u)]
        ds[0] = dot3(fh[:, taps:], fl[:, taps:], xh[taps:, :], xl[taps:, :])
        spectrum_product(hs, k, ds, 0, -1)
        w1b[k, 16 : 16 + length] = dot3(ih[...], il[...], xh[...], xl[...])
        value_sums = [jnp.zeros((8, chans), F32) for _ in range(3)]
        for r in range(0, length, 32):
            w1 = w1b[k, 16 + r : 48 + r]
            u = delayed(k, r, 32)
            value_sums = [s + fold(w1 * d) for s, d in zip(value_sums, u)]
        for i, s in enumerate(gate_sums + value_sums):
            ext[i : i + 1] = jnp.sum(s, axis=0, keepdims=True) * scale
        ext[6:8] = jnp.zeros((2, chans), F32)
        spectrum_product(vs, k, ds, 0, -1)
        part[0:taps] = dot3(ih[0:taps, :], il[0:taps, :], xh[...], xl[...]) * scale
        part[taps : taps + EXTRA] = ext[...]
        if k == 0:
            sent = remote(part, part_in, one_send.at[0], one_recv.at[0], partner, tp)
            sent.start()
            input_gradient(k)
            sent.wait_send()

    finish(part_in, one_recv.at[0])
    extra_total = part[taps : taps + EXTRA] + part_in[taps : taps + EXTRA]
    for s in range(xs):
        rows_of = slice(s * slice_rows, (s + 1) * slice_rows)
        rs[s, 0:slice_rows] = part[rows_of] + part_in[rows_of]
        rs[s, slice_rows : slice_rows + EXTRA] = extra_total
    loop(
        xs,
        lambda i: remote(
            rs.at[x_peer(i)], xr.at[x], one_send.at[1], one_recv.at[1], x_ctx(x_peer(i)), tp
        ).start(),
    )
    xr[x] = rs[x]
    input_gradient(1)
    finish(xr.at[pl.ds(0, xs - 1)], one_recv.at[1])
    total = xr[0]
    for s in range(1, xs):
        total = total + xr[s]
    yr[ylo] = total
    loop(
        ys,
        lambda i: remote(
            yr.at[ylo], yr.at[ylo], one_send.at[2], one_recv.at[2], y_ctx(i), tp
        ).start(),
    )

    @pl.when(ctx < nctx - 1)
    def _():
        for k in range(2):
            finish(head_in.at[k], head_recv.at[k])

    for k in range(2):
        for r in range(0, tokens, 16):
            block = igb[k, r : r + 16]
            late = r - (tokens - halo)
            if late >= 0:
                block = block + head_in[k, late : late + 16].astype(F32)
            ig_out[r : r + 16, pl.ds(offset(k), chans)] = block.astype(BF16)

    finish(yr.at[pl.ds(0, ys - 1)], one_recv.at[2])
    total = yr[0]
    for s in range(1, ys):
        total = total + yr[s]
    slot = core * xs + x
    ag[slot] = total[0:slice_rows]
    ext[...] = total[slice_rows : slice_rows + EXTRA]
    loop(
        2 * xs,
        lambda i: remote(
            ag.at[slot], ag.at[slot], one_send.at[3], one_recv.at[3], row_peer(i), tp
        ).start(),
    )
    remote(ext, ext_in, one_send.at[4], one_recv.at[4], partner, tp).start()
    gate_out[:, pl.ds(offset(1), chans)] = ext[0:3]
    value_out[:, pl.ds(offset(1), chans)] = ext[3:6]
    finish(ext_in, one_recv.at[4])
    gate_out[:, pl.ds(offset(0), chans)] = ext_in[0:3]
    value_out[:, pl.ds(offset(0), chans)] = ext_in[3:6]
    finish(ag.at[pl.ds(0, 2 * xs - 1)], one_recv.at[3])
    for half in range(2):
        for s in range(xs):
            efg_out[
                s * slice_rows : (s + 1) * slice_rows, half * chans : (half + 1) * chans
            ] = ag[half * xs + s]

    for k in range(2):
        finish(ubuf.at[k, pl.ds(0, rows * (ntp - 1)), :], a2a_send.at[k])
        finish(gbuf.at[k, pl.ds(0, rows * (ntp - 1)), :], a2a_send.at[2 + k])

        @pl.when(ctx < nctx - 1)
        def _(k=k):
            finish(ubuf.at[k, pl.ds(0, halo), :], halo_send.at[k])

        @pl.when(ctx > 0)
        def _(k=k):
            finish(head.at[k], head_send.at[k])

    finish(rs.at[pl.ds(0, xs - 1)], one_send.at[1])
    finish(yr.at[pl.ds(0, ys - 1)], one_send.at[2])
    finish(ag.at[pl.ds(0, 2 * xs - 1)], one_send.at[3])
    finish(ext, one_send.at[4])


def shards(mesh, out_grad, saved_input, explicit_filter_weights, gate_taps, value_featurizer_weights):
    nctx, ntp = mesh.shape["ctx"], mesh.shape["tp"]
    rows, channels = out_grad.shape
    width = channels // ntp
    tokens = rows * ntp
    taps = explicit_filter_weights.shape[0]
    xs = 8 if nctx >= 64 else 2
    ys = nctx // (2 * xs)
    chans = width // 2
    halo = -(-(taps + gate_taps.shape[0] - 2) // 16) * 16
    length = tokens + taps
    slice_rows = taps // xs
    scale = np.float32(1.0 / math.sqrt(tokens * nctx))
    matrices = [jnp.asarray(m) for m in transforms(length)]
    anywhere = pl.BlockSpec(memory_space=pl.ANY)
    vmem = pl.BlockSpec(memory_space=pltpu.VMEM)
    scratch = [
        pltpu.VMEM((2, halo + tokens, chans), BF16),
        pltpu.VMEM((2, tokens, chans), BF16),
        pltpu.VMEM((2, taps, chans), F32),
        *[pltpu.VMEM((length, length), BF16) for _ in range(4)],
        pltpu.VMEM((2, length, chans), F32),
        pltpu.VMEM((2, length, chans), F32),
        pltpu.VMEM((1, length, chans), F32),
        pltpu.VMEM((2, halo + tokens, chans), F32),
        pltpu.VMEM((2, tokens, chans), F32),
        pltpu.VMEM((2, tokens, chans), F32),
        pltpu.VMEM((length, chans), BF16),
        pltpu.VMEM((length, chans), BF16),
        pltpu.VMEM((2, length + 32, chans), F32),
        pltpu.VMEM((2, tokens + 32, chans), F32),
        pltpu.VMEM((2, tokens, chans), F32),
        pltpu.VMEM((2, halo, chans), BF16),
        pltpu.VMEM((2, halo, chans), BF16),
        pltpu.VMEM((taps + EXTRA, chans), F32),
        pltpu.VMEM((taps + EXTRA, chans), F32),
        pltpu.VMEM((EXTRA, chans), F32),
        pltpu.VMEM((xs, slice_rows + EXTRA, chans), F32),
        pltpu.VMEM((xs, slice_rows + EXTRA, chans), F32),
        pltpu.VMEM((ys, slice_rows + EXTRA, chans), F32),
        pltpu.VMEM((2 * xs, slice_rows, chans), F32),
        pltpu.VMEM((EXTRA, chans), F32),
        pltpu.SemaphoreType.DMA((4,)),
        pltpu.SemaphoreType.DMA((4,)),
        pltpu.SemaphoreType.DMA((2,)),
        pltpu.SemaphoreType.DMA((2,)),
        pltpu.SemaphoreType.DMA((2,)),
        pltpu.SemaphoreType.DMA((2,)),
        pltpu.SemaphoreType.DMA((6,)),
        pltpu.SemaphoreType.DMA((5,)),
        pltpu.SemaphoreType.DMA((5,)),
    ]
    return pl.pallas_call(
        functools.partial(kernel, (nctx, ntp, xs, ys, taps, scale)),
        out_shape=(
            jax.ShapeDtypeStruct((tokens, width), BF16),
            jax.ShapeDtypeStruct((taps, width), F32),
            jax.ShapeDtypeStruct(gate_taps.shape, F32),
            jax.ShapeDtypeStruct(value_featurizer_weights.shape, F32),
        ),
        in_specs=[anywhere, anywhere, anywhere, vmem, vmem] + [anywhere] * 4,
        out_specs=(vmem, vmem, vmem, vmem),
        scratch_shapes=scratch,
        compiler_params=pltpu.CompilerParams(
            collective_id=0, has_side_effects=True, vmem_limit_bytes=48 * 2**20
        ),
    )(
        out_grad, saved_input, explicit_filter_weights, gate_taps, value_featurizer_weights,
        *matrices,
    )


def solution(mesh):
    placed = (
        P(("ctx", "tp"), None),
        P(("ctx", "tp"), None),
        P(None, "tp"),
        P(None, "tp"),
        P(None, "tp"),
    )
    return jax.shard_map(
        functools.partial(shards, mesh),
        mesh=mesh,
        in_specs=placed,
        out_specs=(P("ctx", "tp"), P(None, "tp"), P(None, "tp"), P(None, "tp")),
        check_vma=False,
    )
```

```python
import functools
import math

import jax
import jax.numpy as jnp
import ml_dtypes
import numpy as np
from jax import lax
from jax.experimental import pallas as pl
from jax.experimental.pallas import tpu as pltpu
from jax.sharding import PartitionSpec as P

MESH = pl.DeviceIdType.MESH
F32 = jnp.float32
BF16 = jnp.bfloat16
EXTRA = 8


def two_parts(matrix):
    high = matrix.astype(ml_dtypes.bfloat16)
    low = (matrix - high.astype(np.float64)).astype(ml_dtypes.bfloat16)
    return high, low


def transforms(length):
    odd = 2 * np.arange(length // 2)[:, None] + 1
    steps = (odd * np.arange(length)[None, :]) % (2 * length)
    angle = np.pi * steps / length
    forward = np.concatenate([np.cos(angle), -np.sin(angle)])
    inverse = forward.T * (2.0 / length)
    return two_parts(forward) + two_parts(inverse)


def split(x):
    high = x.astype(BF16)
    return high, (x - high.astype(F32)).astype(BF16)


def dot3(ah, al, xh, xl):
    def dot(a, b):
        return jnp.dot(a, b, preferred_element_type=F32)

    return dot(ah, xh) + dot(ah, xl) + dot(al, xh)


def kernel(
    sizes,
    og, si, h_hbm, gt_hbm, w_hbm, fh_hbm, fl_hbm, ih_hbm, il_hbm,
    ig_out, efg_out, gate_out, value_out,
    ubuf, gbuf, hb, fh, fl, ih, il,
    hs, vs, ds, uf, qb, zb, xh, xl, w1b, dqb, igb, head, head_in,
    part, part_in, ext, rs, xr, yr, ag, ext_in, gt_ref, w_ref,
    a2a_send, a2a_recv, halo_send, halo_recv, head_send, head_recv,
    const_sem, one_send, one_recv,
):
    nctx, ntp, xs, ys, taps, scale = sizes
    rows, width = og.shape[0], og.shape[1] // ntp
    tokens = rows * ntp
    chans = width // 2
    halo = ubuf.shape[1] - tokens
    length = tokens + taps
    half_len = length // 2
    slice_rows = taps // xs
    ctx, tp = lax.axis_index("ctx"), lax.axis_index("tp")
    core = lax.rem(ctx, 2)
    x = lax.rem(ctx // 2, xs)
    ylo = ctx // (2 * xs)
    row16 = lax.rem(ctx, 2 * xs)

    def remote(src, dst, send, recv, to_ctx, to_tp):
        return pltpu.make_async_remote_copy(
            src_ref=src, dst_ref=dst, send_sem=send, recv_sem=recv,
            device_id=(to_ctx, to_tp), device_id_type=MESH,
        )

    def finish(ref, sem):
        pltpu.make_async_copy(ref, ref, sem).wait()

    def offset(k):
        half = (1 - core) if k == 0 else core
        return pl.multiple_of(half * chans, chans)

    def tp_peer(i):
        return lax.rem(tp + i, ntp)

    def row_peer(i):
        return ylo * (2 * xs) + lax.rem(row16 + i, 2 * xs)

    def x_peer(i):
        return lax.rem(x + i, xs)

    def x_ctx(other):
        return (ylo * xs + other) * 2 + core

    def y_ctx(i):
        return (lax.rem(ylo + i, ys) * xs + x) * 2 + core

    barrier = pltpu.get_barrier_semaphore()

    def greet(to_ctx, to_tp):
        pl.semaphore_signal(barrier, inc=1, device_id=(to_ctx, to_tp), device_id_type=MESH)

    def loop(count, body):
        def step(i, carry):
            body(i)
            return carry

        lax.fori_loop(1, count, step, 0)

    loop(ntp, lambda i: greet(ctx, tp_peer(i)))
    loop(2 * xs, lambda i: greet(row_peer(i), tp))
    loop(ys, lambda i: greet(y_ctx(i), tp))

    @pl.when(ctx > 0)
    def _():
        greet(ctx - 1, tp)

    @pl.when(ctx < nctx - 1)
    def _():
        greet(ctx + 1, tp)

    constants = [
        pltpu.make_async_copy(src, dst, const_sem.at[i])
        for i, (src, dst) in enumerate(
            [(fh_hbm, fh), (fl_hbm, fl), (ih_hbm, ih), (il_hbm, il), (gt_hbm, gt_ref), (w_hbm, w_ref)]
            + [(h_hbm.at[:, pl.ds(offset(k), chans)], hb.at[k]) for k in range(2)]
        )
    ]
    for copy in constants:
        copy.start()

    @pl.when(ctx == 0)
    def _():
        ubuf[:, 0:halo, :] = jnp.zeros((2, halo, chans), BF16)

    @pl.when(ctx == nctx - 1)
    def _():
        head_in[...] = jnp.zeros(head_in.shape, BF16)

    greeted = ntp - 1 + 2 * xs - 1 + ys - 1
    greeted = greeted + jnp.where(ctx > 0, 1, 0) + jnp.where(ctx < nctx - 1, 1, 0)
    pl.semaphore_wait(barrier, greeted)

    def exchange(src, dst, base, k, sem):
        def columns(who):
            return src.at[:, pl.ds(pl.multiple_of(who * width + offset(k), chans), chans)]

        place = dst.at[k, pl.ds(pl.multiple_of(base + tp * rows, 16), rows), :]
        loop(
            ntp,
            lambda i: remote(
                columns(tp_peer(i)), place, a2a_send.at[sem], a2a_recv.at[sem], ctx, tp_peer(i)
            ).start(),
        )
        pltpu.make_async_copy(columns(tp), place, a2a_recv.at[sem]).start()

    exchange(si, ubuf, halo, 0, 0)
    exchange(si, ubuf, halo, 1, 1)
    exchange(og, gbuf, 0, 0, 2)
    exchange(og, gbuf, 0, 1, 3)

    for copy in constants:
        copy.wait()
    for k in range(2):
        th, tl = split(hb[k])
        hs[k] = dot3(fh[:, 0:taps], fl[:, 0:taps], th, tl)
    w1b[:, 0:16, :] = jnp.zeros((2, 16, chans), F32)
    w1b[:, 16 + length : 32 + length, :] = jnp.zeros((2, 16, chans), F32)
    dqb[:, 0:16, :] = jnp.zeros((2, 16, chans), F32)
    dqb[:, 16 + tokens : 32 + tokens, :] = jnp.zeros((2, 16, chans), F32)

    def taps_of(ref, k):
        block = ref[:, pl.ds(offset(k), chans)]
        return [block[i : i + 1] for i in range(3)]

    def halo_copy(k):
        return remote(
            ubuf.at[k, pl.ds(tokens, halo), :], ubuf.at[1 - k, pl.ds(0, halo), :],
            halo_send.at[k], halo_recv.at[1 - k], ctx + 1, tp,
        )

    for k in range(2):
        finish(ubuf.at[k, pl.ds(halo, tokens), :], a2a_recv.at[k])

        @pl.when(ctx < nctx - 1)
        def _(k=k):
            halo_copy(k).start()

    def spectrum_product(a, a_k, b, b_k, sign):
        for r in range(0, half_len, 32):
            ar, ai = a[a_k, r : r + 32], a[a_k, half_len + r : half_len + r + 32]
            br, bi = b[b_k, r : r + 32], b[b_k, half_len + r : half_len + r + 32]
            if sign > 0:
                re, im = ar * br - ai * bi, ar * bi + ai * br
            else:
                re, im = ar * br + ai * bi, ar * bi - ai * br
            xh[r : r + 32], xl[r : r + 32] = split(re)
            xh[half_len + r : half_len + r + 32], xl[half_len + r : half_len + r + 32] = split(im)

    def delayed(k, r, count):
        first = halo - taps + r
        return [uf[k, first - i : first - i + count] for i in range(3)]

    for k in range(2):

        @pl.when(ctx > 0)
        def _(k=k):
            finish(ubuf.at[k, pl.ds(0, halo), :], halo_recv.at[k])

        for r in range(0, halo + tokens, 16):
            uf[k, r : r + 16] = ubuf[k, r : r + 16].astype(F32)
        wv, wg = taps_of(w_ref, k), taps_of(gt_ref, k)
        for r in range(0, length, 32):
            u = delayed(k, r, 32)
            v = wv[0] * u[0] + wv[1] * u[1] + wv[2] * u[2]
            xh[r : r + 32], xl[r : r + 32] = split(v)
            if r >= taps:
                qb[k, r - taps : r - taps + 32] = wg[0] * u[0] + wg[1] * u[1] + wg[2] * u[2]
        vs[k] = dot3(fh[...], fl[...], xh[...], xl[...])
        spectrum_product(hs, k, vs, k, 1)
        zb[k] = dot3(ih[taps:, :], il[taps:, :], xh[...], xl[...])

    def fold(values):
        return jnp.sum(values.reshape(values.shape[0] // 8, 8, chans), axis=0)

    def input_gradient(k):
        wv, wg = taps_of(w_ref, k), taps_of(gt_ref, k)
        for r in range(0, halo + tokens, 16):
            a = [w1b[k, r + i : r + i + 16] for i in range(3)]
            total = wv[0] * a[0] + wv[1] * a[1] + wv[2] * a[2]
            first = r - halo
            if first >= -16:
                d = [dqb[k, 16 + first + i : 32 + first + i] for i in range(3)]
                total = total + wg[0] * d[0] + wg[1] * d[1] + wg[2] * d[2]
            if first < 0:
                head[k, r : r + 16] = total.astype(BF16)
            else:
                igb[k, first : first + 16] = total

        @pl.when(ctx > 0)
        def _():
            remote(
                head.at[k], head_in.at[1 - k], head_send.at[k], head_recv.at[1 - k], ctx - 1, tp
            ).start()

    partner = ctx + 1 - 2 * core

    for k in range(2):
        finish(gbuf.at[k], a2a_recv.at[2 + k])
        gate_sums = [jnp.zeros((8, chans), F32) for _ in range(3)]
        for r in range(0, tokens, 32):
            g = gbuf[k, r : r + 32].astype(F32)
            xh[taps + r : taps + r + 32], xl[taps + r : taps + r + 32] = split(
                g * qb[k, r : r + 32]
            )
            dq = g * zb[k, r : r + 32]
            dqb[k, 16 + r : 48 + r] = dq
            u = delayed(k, taps + r, 32)
            gate_sums = [s + fold(dq * d) for s, d in zip(gate_sums, u)]
        ds[0] = dot3(fh[:, taps:], fl[:, taps:], xh[taps:, :], xl[taps:, :])
        spectrum_product(hs, k, ds, 0, -1)
        w1b[k, 16 : 16 + length] = dot3(ih[...], il[...], xh[...], xl[...])
        value_sums = [jnp.zeros((8, chans), F32) for _ in range(3)]
        for r in range(0, length, 32):
            w1 = w1b[k, 16 + r : 48 + r]
            u = delayed(k, r, 32)
            value_sums = [s + fold(w1 * d) for s, d in zip(value_sums, u)]
        for i, s in enumerate(gate_sums + value_sums):
            ext[i : i + 1] = jnp.sum(s, axis=0, keepdims=True) * scale
        ext[6:8] = jnp.zeros((2, chans), F32)
        spectrum_product(vs, k, ds, 0, -1)
        part[0:taps] = dot3(ih[0:taps, :], il[0:taps, :], xh[...], xl[...]) * scale
        part[taps : taps + EXTRA] = ext[...]
        if k == 0:
            sent = remote(part, part_in, one_send.at[0], one_recv.at[0], partner, tp)
            sent.start()
            input_gradient(k)
            sent.wait_send()

    finish(part_in, one_recv.at[0])
    extra_total = part[taps : taps + EXTRA] + part_in[taps : taps + EXTRA]
    for s in range(xs):
        rows_of = slice(s * slice_rows, (s + 1) * slice_rows)
        rs[s, 0:slice_rows] = part[rows_of] + part_in[rows_of]
        rs[s, slice_rows : slice_rows + EXTRA] = extra_total
    loop(
        xs,
        lambda i: remote(
            rs.at[x_peer(i)], xr.at[x], one_send.at[1], one_recv.at[1], x_ctx(x_peer(i)), tp
        ).start(),
    )
    xr[x] = rs[x]
    input_gradient(1)
    finish(xr.at[pl.ds(0, xs - 1)], one_recv.at[1])
    total = xr[0]
    for s in range(1, xs):
        total = total + xr[s]
    yr[ylo] = total
    loop(
        ys,
        lambda i: remote(
            yr.at[ylo], yr.at[ylo], one_send.at[2], one_recv.at[2], y_ctx(i), tp
        ).start(),
    )

    @pl.when(ctx < nctx - 1)
    def _():
        for k in range(2):
            finish(head_in.at[k], head_recv.at[k])

    for k in range(2):
        for r in range(0, tokens, 16):
            block = igb[k, r : r + 16]
            late = r - (tokens - halo)
            if late >= 0:
                block = block + head_in[k, late : late + 16].astype(F32)
            ig_out[r : r + 16, pl.ds(offset(k), chans)] = block.astype(BF16)

    finish(yr.at[pl.ds(0, ys - 1)], one_recv.at[2])
    total = yr[0]
    for s in range(1, ys):
        total = total + yr[s]
    slot = core * xs + x
    ag[slot] = total[0:slice_rows]
    ext[...] = total[slice_rows : slice_rows + EXTRA]
    loop(
        2 * xs,
        lambda i: remote(
            ag.at[slot], ag.at[slot], one_send.at[3], one_recv.at[3], row_peer(i), tp
        ).start(),
    )
    remote(ext, ext_in, one_send.at[4], one_recv.at[4], partner, tp).start()
    gate_out[:, pl.ds(offset(1), chans)] = ext[0:3]
    value_out[:, pl.ds(offset(1), chans)] = ext[3:6]
    finish(ext_in, one_recv.at[4])
    gate_out[:, pl.ds(offset(0), chans)] = ext_in[0:3]
    value_out[:, pl.ds(offset(0), chans)] = ext_in[3:6]
    finish(ag.at[pl.ds(0, 2 * xs - 1)], one_recv.at[3])
    for half in range(2):
        for s in range(xs):
            efg_out[
                s * slice_rows : (s + 1) * slice_rows, half * chans : (half + 1) * chans
            ] = ag[half * xs + s]

    for k in range(2):
        finish(ubuf.at[k, pl.ds(0, rows * (ntp - 1)), :], a2a_send.at[k])
        finish(gbuf.at[k, pl.ds(0, rows * (ntp - 1)), :], a2a_send.at[2 + k])

        @pl.when(ctx < nctx - 1)
        def _(k=k):
            finish(ubuf.at[k, pl.ds(0, halo), :], halo_send.at[k])

        @pl.when(ctx > 0)
        def _(k=k):
            finish(head.at[k], head_send.at[k])

    finish(rs.at[pl.ds(0, xs - 1)], one_send.at[1])
    finish(yr.at[pl.ds(0, ys - 1)], one_send.at[2])
    finish(ag.at[pl.ds(0, 2 * xs - 1)], one_send.at[3])
    finish(ext, one_send.at[4])


def write_out(*refs):
    copies = [
        pltpu.make_async_copy(refs[i], refs[4 + i], refs[8].at[i]) for i in range(4)
    ]
    for copy in copies:
        copy.start()
    for copy in copies:
        copy.wait()


def shards(mesh, out_grad, saved_input, explicit_filter_weights, gate_taps, value_featurizer_weights):
    nctx, ntp = mesh.shape["ctx"], mesh.shape["tp"]
    rows, channels = out_grad.shape
    width = channels // ntp
    tokens = rows * ntp
    taps = explicit_filter_weights.shape[0]
    xs = 8 if nctx >= 64 else 2
    ys = nctx // (2 * xs)
    chans = width // 2
    halo = -(-(taps + gate_taps.shape[0] - 2) // 16) * 16
    length = tokens + taps
    slice_rows = taps // xs
    scale = np.float32(1.0 / math.sqrt(tokens * nctx))
    matrices = [jnp.asarray(m) for m in transforms(length)]
    hbm = pl.BlockSpec(memory_space=pltpu.HBM)
    vmem = pl.BlockSpec(memory_space=pltpu.VMEM)
    scratch = [
        pltpu.VMEM((2, halo + tokens, chans), BF16),
        pltpu.VMEM((2, tokens, chans), BF16),
        pltpu.VMEM((2, taps, chans), F32),
        *[pltpu.VMEM((length, length), BF16) for _ in range(4)],
        pltpu.VMEM((2, length, chans), F32),
        pltpu.VMEM((2, length, chans), F32),
        pltpu.VMEM((1, length, chans), F32),
        pltpu.VMEM((2, halo + tokens, chans), F32),
        pltpu.VMEM((2, tokens, chans), F32),
        pltpu.VMEM((2, tokens, chans), F32),
        pltpu.VMEM((length, chans), BF16),
        pltpu.VMEM((length, chans), BF16),
        pltpu.VMEM((2, length + 32, chans), F32),
        pltpu.VMEM((2, tokens + 32, chans), F32),
        pltpu.VMEM((2, tokens, chans), F32),
        pltpu.VMEM((2, halo, chans), BF16),
        pltpu.VMEM((2, halo, chans), BF16),
        pltpu.VMEM((taps + EXTRA, chans), F32),
        pltpu.VMEM((taps + EXTRA, chans), F32),
        pltpu.VMEM((EXTRA, chans), F32),
        pltpu.VMEM((xs, slice_rows + EXTRA, chans), F32),
        pltpu.VMEM((xs, slice_rows + EXTRA, chans), F32),
        pltpu.VMEM((ys, slice_rows + EXTRA, chans), F32),
        pltpu.VMEM((2 * xs, slice_rows, chans), F32),
        pltpu.VMEM((EXTRA, chans), F32),
        pltpu.VMEM(gate_taps.shape, F32),
        pltpu.VMEM(value_featurizer_weights.shape, F32),
        pltpu.SemaphoreType.DMA((4,)),
        pltpu.SemaphoreType.DMA((4,)),
        pltpu.SemaphoreType.DMA((2,)),
        pltpu.SemaphoreType.DMA((2,)),
        pltpu.SemaphoreType.DMA((2,)),
        pltpu.SemaphoreType.DMA((2,)),
        pltpu.SemaphoreType.DMA((8,)),
        pltpu.SemaphoreType.DMA((5,)),
        pltpu.SemaphoreType.DMA((5,)),
    ]
    results = pl.pallas_call(
        functools.partial(kernel, (nctx, ntp, xs, ys, taps, scale)),
        out_shape=(
            jax.ShapeDtypeStruct((tokens, width), BF16),
            jax.ShapeDtypeStruct((taps, width), F32),
            jax.ShapeDtypeStruct(gate_taps.shape, F32),
            jax.ShapeDtypeStruct(value_featurizer_weights.shape, F32),
        ),
        in_specs=[hbm] * 9,
        out_specs=(vmem, vmem, vmem, vmem),
        scratch_shapes=scratch,
        compiler_params=pltpu.CompilerParams(
            collective_id=0, has_side_effects=True, vmem_limit_bytes=55_900_000
        ),
    )(
        out_grad, saved_input, explicit_filter_weights, gate_taps, value_featurizer_weights,
        *matrices,
    )
    return pl.pallas_call(
        write_out,
        out_shape=[jax.ShapeDtypeStruct(r.shape, r.dtype) for r in results],
        in_specs=[vmem] * 4,
        out_specs=[hbm] * 4,
        scratch_shapes=[pltpu.SemaphoreType.DMA((4,))],
        compiler_params=pltpu.CompilerParams(vmem_limit_bytes=2**20),
    )(*results)


def solution(mesh):
    placed = (
        P(("ctx", "tp"), None),
        P(("ctx", "tp"), None),
        P(None, "tp"),
        P(None, "tp"),
        P(None, "tp"),
    )
    return jax.shard_map(
        functools.partial(shards, mesh),
        mesh=mesh,
        in_specs=placed,
        out_specs=(P("ctx", "tp"), P(None, "tp"), P(None, "tp"), P(None, "tp")),
        check_vma=False,
    )
```

```python
import functools
import math

import jax
import jax.numpy as jnp
import ml_dtypes
import numpy as np
from jax import lax
from jax.experimental import pallas as pl
from jax.experimental.pallas import tpu as pltpu
from jax.sharding import PartitionSpec as P

MESH = pl.DeviceIdType.MESH
F32 = jnp.float32
BF16 = jnp.bfloat16
EXTRA = 8


def two_parts(matrix):
    high = matrix.astype(ml_dtypes.bfloat16)
    low = (matrix - high.astype(np.float64)).astype(ml_dtypes.bfloat16)
    return high, low


def transforms(length):
    odd = 2 * np.arange(length // 2)[:, None] + 1
    steps = (odd * np.arange(length)[None, :]) % (2 * length)
    angle = np.pi * steps / length
    forward = np.concatenate([np.cos(angle), -np.sin(angle)])
    inverse = forward.T * (2.0 / length)
    return two_parts(forward) + two_parts(inverse)


def split(x):
    high = x.astype(BF16)
    return high, (x - high.astype(F32)).astype(BF16)


def dot3(ah, al, xh, xl):
    def dot(a, b):
        return jnp.dot(a, b, preferred_element_type=F32)

    return dot(ah, xh) + dot(ah, xl) + dot(al, xh)


def kernel(
    sizes,
    og, si, h_hbm, gt_hbm, w_hbm, fh_hbm, fl_hbm, ih_hbm, il_hbm,
    ig_out, efg_out, gate_out, value_out,
    ubuf, gbuf, hb, fh, fl, ih, il,
    hs, vs, ds, uf, qb, zb, xh, xl, w1b, dqb, igb, head, head_in,
    part, part_in, ext, ext_in, rs, xr, xe, yr, ye, ag, gt_ref, w_ref,
    a2a_send, a2a_recv, halo_send, halo_recv, head_send, head_recv,
    const_sem, one_send, one_recv,
):
    nctx, ntp, xs, ys, taps, scale = sizes
    rows, width = og.shape[0], og.shape[1] // ntp
    tokens = rows * ntp
    chans = width // 2
    halo = ubuf.shape[1] - tokens
    length = tokens + taps
    half_len = length // 2
    slice_rows = taps // xs
    ctx, tp = lax.axis_index("ctx"), lax.axis_index("tp")
    core = lax.rem(ctx, 2)
    x = lax.rem(ctx // 2, xs)
    ylo = ctx // (2 * xs)
    row16 = lax.rem(ctx, 2 * xs)

    def remote(src, dst, send, recv, to_ctx, to_tp):
        return pltpu.make_async_remote_copy(
            src_ref=src, dst_ref=dst, send_sem=send, recv_sem=recv,
            device_id=(to_ctx, to_tp), device_id_type=MESH,
        )

    def finish(ref, sem):
        pltpu.make_async_copy(ref, ref, sem).wait()

    def offset(k):
        half = (1 - core) if k == 0 else core
        return pl.multiple_of(half * chans, chans)

    def tp_peer(i):
        return lax.rem(tp + i, ntp)

    def row_peer(i):
        return ylo * (2 * xs) + lax.rem(row16 + i, 2 * xs)

    def x_peer(i):
        return lax.rem(x + i, xs)

    def x_ctx(other):
        return (ylo * xs + other) * 2 + core

    def y_ctx(i):
        return (lax.rem(ylo + i, ys) * xs + x) * 2 + core

    barrier = pltpu.get_barrier_semaphore()

    def greet(to_ctx, to_tp):
        pl.semaphore_signal(barrier, inc=1, device_id=(to_ctx, to_tp), device_id_type=MESH)

    def loop(count, body):
        def step(i, carry):
            body(i)
            return carry

        lax.fori_loop(1, count, step, 0)

    loop(ntp, lambda i: greet(ctx, tp_peer(i)))
    loop(2 * xs, lambda i: greet(row_peer(i), tp))
    loop(ys, lambda i: greet(y_ctx(i), tp))

    @pl.when(ctx > 0)
    def _():
        greet(ctx - 1, tp)

    @pl.when(ctx < nctx - 1)
    def _():
        greet(ctx + 1, tp)

    constants = [
        pltpu.make_async_copy(src, dst, const_sem.at[i])
        for i, (src, dst) in enumerate(
            [(fh_hbm, fh), (fl_hbm, fl), (ih_hbm, ih), (il_hbm, il), (gt_hbm, gt_ref), (w_hbm, w_ref)]
            + [(h_hbm.at[:, pl.ds(offset(k), chans)], hb.at[k]) for k in range(2)]
        )
    ]
    for copy in constants:
        copy.start()

    @pl.when(ctx == 0)
    def _():
        ubuf[:, 0:halo, :] = jnp.zeros((2, halo, chans), BF16)

    @pl.when(ctx == nctx - 1)
    def _():
        head_in[...] = jnp.zeros(head_in.shape, BF16)

    greeted = ntp - 1 + 2 * xs - 1 + ys - 1
    greeted = greeted + jnp.where(ctx > 0, 1, 0) + jnp.where(ctx < nctx - 1, 1, 0)
    pl.semaphore_wait(barrier, greeted)

    def exchange(src, dst, base, k, sem):
        def columns(who):
            return src.at[:, pl.ds(pl.multiple_of(who * width + offset(k), chans), chans)]

        place = dst.at[k, pl.ds(pl.multiple_of(base + tp * rows, 16), rows), :]
        loop(
            ntp,
            lambda i: remote(
                columns(tp_peer(i)), place, a2a_send.at[sem], a2a_recv.at[sem], ctx, tp_peer(i)
            ).start(),
        )
        pltpu.make_async_copy(columns(tp), place, a2a_recv.at[sem]).start()

    exchange(si, ubuf, halo, 0, 0)
    exchange(si, ubuf, halo, 1, 1)
    exchange(og, gbuf, 0, 0, 2)
    exchange(og, gbuf, 0, 1, 3)

    for copy in constants:
        copy.wait()
    for k in range(2):
        th, tl = split(hb[k])
        hs[k] = dot3(fh[:, 0:taps], fl[:, 0:taps], th, tl)
    w1b[:, 0:16, :] = jnp.zeros((2, 16, chans), F32)
    w1b[:, 16 + length : 32 + length, :] = jnp.zeros((2, 16, chans), F32)
    dqb[:, 0:16, :] = jnp.zeros((2, 16, chans), F32)
    dqb[:, 16 + tokens : 32 + tokens, :] = jnp.zeros((2, 16, chans), F32)

    def taps_of(ref, k):
        block = ref[:, pl.ds(offset(k), chans)]
        return [block[i : i + 1] for i in range(3)]

    def halo_copy(k):
        return remote(
            ubuf.at[k, pl.ds(tokens, halo), :], ubuf.at[1 - k, pl.ds(0, halo), :],
            halo_send.at[k], halo_recv.at[1 - k], ctx + 1, tp,
        )

    for k in range(2):
        finish(ubuf.at[k, pl.ds(halo, tokens), :], a2a_recv.at[k])

        @pl.when(ctx < nctx - 1)
        def _(k=k):
            halo_copy(k).start()

    def spectrum_product(a, a_k, b, b_k, sign):
        for r in range(0, half_len, 32):
            ar, ai = a[a_k, r : r + 32], a[a_k, half_len + r : half_len + r + 32]
            br, bi = b[b_k, r : r + 32], b[b_k, half_len + r : half_len + r + 32]
            if sign > 0:
                re, im = ar * br - ai * bi, ar * bi + ai * br
            else:
                re, im = ar * br + ai * bi, ar * bi - ai * br
            xh[r : r + 32], xl[r : r + 32] = split(re)
            xh[half_len + r : half_len + r + 32], xl[half_len + r : half_len + r + 32] = split(im)

    def delayed(k, r, count):
        first = halo - taps + r
        return [uf[k, first - i : first - i + count] for i in range(3)]

    for k in range(2):

        @pl.when(ctx > 0)
        def _(k=k):
            finish(ubuf.at[k, pl.ds(0, halo), :], halo_recv.at[k])

        for r in range(0, halo + tokens, 16):
            uf[k, r : r + 16] = ubuf[k, r : r + 16].astype(F32)
        wv, wg = taps_of(w_ref, k), taps_of(gt_ref, k)
        for r in range(0, length, 32):
            u = delayed(k, r, 32)
            v = wv[0] * u[0] + wv[1] * u[1] + wv[2] * u[2]
            xh[r : r + 32], xl[r : r + 32] = split(v)
            if r >= taps:
                qb[k, r - taps : r - taps + 32] = wg[0] * u[0] + wg[1] * u[1] + wg[2] * u[2]
        vs[k] = dot3(fh[...], fl[...], xh[...], xl[...])
        spectrum_product(hs, k, vs, k, 1)
        zb[k] = dot3(ih[taps:, :], il[taps:, :], xh[...], xl[...])

    def fold(values):
        return jnp.sum(values.reshape(values.shape[0] // 8, 8, chans), axis=0)

    def input_gradient(k):
        wv, wg = taps_of(w_ref, k), taps_of(gt_ref, k)
        for r in range(0, halo + tokens, 16):
            a = [w1b[k, r + i : r + i + 16] for i in range(3)]
            total = wv[0] * a[0] + wv[1] * a[1] + wv[2] * a[2]
            first = r - halo
            if first >= -16:
                d = [dqb[k, 16 + first + i : 32 + first + i] for i in range(3)]
                total = total + wg[0] * d[0] + wg[1] * d[1] + wg[2] * d[2]
            if first < 0:
                head[k, r : r + 16] = total.astype(BF16)
            else:
                igb[k, first : first + 16] = total

        @pl.when(ctx > 0)
        def _():
            remote(
                head.at[k], head_in.at[1 - k], head_send.at[k], head_recv.at[1 - k], ctx - 1, tp
            ).start()

    partner = ctx + 1 - 2 * core

    for k in range(2):
        finish(gbuf.at[k], a2a_recv.at[2 + k])
        gate_sums = [jnp.zeros((8, chans), F32) for _ in range(3)]
        for r in range(0, tokens, 32):
            g = gbuf[k, r : r + 32].astype(F32)
            xh[taps + r : taps + r + 32], xl[taps + r : taps + r + 32] = split(
                g * qb[k, r : r + 32]
            )
            dq = g * zb[k, r : r + 32]
            dqb[k, 16 + r : 48 + r] = dq
            u = delayed(k, taps + r, 32)
            gate_sums = [s + fold(dq * d) for s, d in zip(gate_sums, u)]
        ds[0] = dot3(fh[:, taps:], fl[:, taps:], xh[taps:, :], xl[taps:, :])
        spectrum_product(vs, k, ds, 0, -1)
        part[0:taps] = dot3(ih[0:taps, :], il[0:taps, :], xh[...], xl[...]) * scale
        if k == 1:
            finish(part_in, one_recv.at[0])
            for s in range(xs):
                rows_of = slice(s * slice_rows, (s + 1) * slice_rows)
                rs[s] = (part[rows_of] + part_in[rows_of]).astype(BF16)
            loop(
                xs,
                lambda i: remote(
                    rs.at[x_peer(i)], xr.at[x], one_send.at[1], one_recv.at[1],
                    x_ctx(x_peer(i)), tp,
                ).start(),
            )
            xr[x] = rs[x]
        spectrum_product(hs, k, ds, 0, -1)
        w1b[k, 16 : 16 + length] = dot3(ih[...], il[...], xh[...], xl[...])
        value_sums = [jnp.zeros((8, chans), F32) for _ in range(3)]
        for r in range(0, length, 32):
            w1 = w1b[k, 16 + r : 48 + r]
            u = delayed(k, r, 32)
            value_sums = [s + fold(w1 * d) for s, d in zip(value_sums, u)]
        for i, s in enumerate(gate_sums + value_sums):
            part[taps + i : taps + i + 1] = jnp.sum(s, axis=0, keepdims=True) * scale
        part[taps + 6 : taps + 8] = jnp.zeros((2, chans), F32)
        if k == 0:
            sent = remote(part, part_in, one_send.at[0], one_recv.at[0], partner, tp)
            sent.start()
            input_gradient(k)
            sent.wait_send()

    own_extra = part[taps : taps + EXTRA] + part_in[taps : taps + EXTRA]
    xe[x] = jnp.concatenate([own_extra[:, : chans // 2], own_extra[:, chans // 2 :]]).astype(BF16)
    loop(
        xs,
        lambda i: remote(
            xe.at[x], xe.at[x], one_send.at[4], one_recv.at[4], x_ctx(x_peer(i)), tp
        ).start(),
    )
    input_gradient(1)
    finish(xr.at[pl.ds(0, xs - 1)], one_recv.at[1])
    total = xr[0].astype(F32)
    for s in range(1, xs):
        total = total + xr[s].astype(F32)
    yr[ylo] = total
    loop(
        ys,
        lambda i: remote(
            yr.at[ylo], yr.at[ylo], one_send.at[2], one_recv.at[2], y_ctx(i), tp
        ).start(),
    )
    finish(xe.at[pl.ds(0, xs - 1)], one_recv.at[4])
    total = xe[0].astype(F32)
    for s in range(1, xs):
        total = total + xe[s].astype(F32)
    ye[ylo] = total
    loop(
        ys,
        lambda i: remote(
            ye.at[ylo], ye.at[ylo], one_send.at[5], one_recv.at[5], y_ctx(i), tp
        ).start(),
    )

    @pl.when(ctx < nctx - 1)
    def _():
        for k in range(2):
            finish(head_in.at[k], head_recv.at[k])

    for k in range(2):
        for r in range(0, tokens, 16):
            block = igb[k, r : r + 16]
            late = r - (tokens - halo)
            if late >= 0:
                block = block + head_in[k, late : late + 16].astype(F32)
            ig_out[r : r + 16, pl.ds(offset(k), chans)] = block.astype(BF16)

    finish(yr.at[pl.ds(0, ys - 1)], one_recv.at[2])
    total = yr[0]
    for s in range(1, ys):
        total = total + yr[s]
    slot = core * xs + x
    ag[slot] = total.astype(BF16)
    loop(
        2 * xs,
        lambda i: remote(
            ag.at[slot], ag.at[slot], one_send.at[3], one_recv.at[3], row_peer(i), tp
        ).start(),
    )
    finish(ye.at[pl.ds(0, ys - 1)], one_recv.at[5])
    total = ye[0]
    for s in range(1, ys):
        total = total + ye[s]
    ext[...] = total
    remote(ext, ext_in, one_send.at[6], one_recv.at[6], partner, tp).start()

    def put_extra(source, k):
        for lane in range(2):
            place = pl.ds(pl.multiple_of(offset(k) + lane * (chans // 2), chans // 2), chans // 2)
            gate_out[:, place] = source[8 * lane : 8 * lane + 3]
            value_out[:, place] = source[8 * lane + 3 : 8 * lane + 6]

    put_extra(ext, 1)
    finish(ext_in, one_recv.at[6])
    put_extra(ext_in, 0)
    finish(ag.at[pl.ds(0, 2 * xs - 1)], one_recv.at[3])
    for half in range(2):
        for s in range(xs):
            efg_out[
                s * slice_rows : (s + 1) * slice_rows, half * chans : (half + 1) * chans
            ] = ag[half * xs + s].astype(F32)

    for k in range(2):
        finish(ubuf.at[k, pl.ds(0, rows * (ntp - 1)), :], a2a_send.at[k])
        finish(gbuf.at[k, pl.ds(0, rows * (ntp - 1)), :], a2a_send.at[2 + k])

        @pl.when(ctx < nctx - 1)
        def _(k=k):
            finish(ubuf.at[k, pl.ds(0, halo), :], halo_send.at[k])

        @pl.when(ctx > 0)
        def _(k=k):
            finish(head.at[k], head_send.at[k])

    finish(rs.at[pl.ds(0, xs - 1)], one_send.at[1])
    finish(yr.at[pl.ds(0, ys - 1)], one_send.at[2])
    finish(ag.at[pl.ds(0, 2 * xs - 1)], one_send.at[3])
    finish(xe.at[pl.ds(0, xs - 1)], one_send.at[4])
    finish(ye.at[pl.ds(0, ys - 1)], one_send.at[5])
    finish(ext, one_send.at[6])


def write_out(*refs):
    copies = [
        pltpu.make_async_copy(refs[i], refs[4 + i], refs[8].at[i]) for i in range(4)
    ]
    for copy in copies:
        copy.start()
    for copy in copies:
        copy.wait()


def shards(mesh, out_grad, saved_input, explicit_filter_weights, gate_taps, value_featurizer_weights):
    nctx, ntp = mesh.shape["ctx"], mesh.shape["tp"]
    rows, channels = out_grad.shape
    width = channels // ntp
    tokens = rows * ntp
    taps = explicit_filter_weights.shape[0]
    xs = 8 if nctx >= 64 else 2
    ys = nctx // (2 * xs)
    chans = width // 2
    halo = -(-(taps + gate_taps.shape[0] - 2) // 16) * 16
    length = tokens + taps
    slice_rows = taps // xs
    scale = np.float32(1.0 / math.sqrt(tokens * nctx))
    matrices = [jnp.asarray(m) for m in transforms(length)]
    hbm = pl.BlockSpec(memory_space=pltpu.HBM)
    vmem = pl.BlockSpec(memory_space=pltpu.VMEM)
    scratch = [
        pltpu.VMEM((2, halo + tokens, chans), BF16),
        pltpu.VMEM((2, tokens, chans), BF16),
        pltpu.VMEM((2, taps, chans), F32),
        *[pltpu.VMEM((length, length), BF16) for _ in range(4)],
        pltpu.VMEM((2, length, chans), F32),
        pltpu.VMEM((2, length, chans), F32),
        pltpu.VMEM((1, length, chans), F32),
        pltpu.VMEM((2, halo + tokens, chans), F32),
        pltpu.VMEM((2, tokens, chans), F32),
        pltpu.VMEM((2, tokens, chans), F32),
        pltpu.VMEM((length, chans), BF16),
        pltpu.VMEM((length, chans), BF16),
        pltpu.VMEM((2, length + 32, chans), F32),
        pltpu.VMEM((2, tokens + 32, chans), F32),
        pltpu.VMEM((2, tokens, chans), F32),
        pltpu.VMEM((2, halo, chans), BF16),
        pltpu.VMEM((2, halo, chans), BF16),
        pltpu.VMEM((taps + EXTRA, chans), F32),
        pltpu.VMEM((taps + EXTRA, chans), F32),
        pltpu.VMEM((2 * EXTRA, chans // 2), F32),
        pltpu.VMEM((2 * EXTRA, chans // 2), F32),
        pltpu.VMEM((xs, slice_rows, chans), BF16),
        pltpu.VMEM((xs, slice_rows, chans), BF16),
        pltpu.VMEM((xs, 2 * EXTRA, chans // 2), BF16),
        pltpu.VMEM((ys, slice_rows, chans), F32),
        pltpu.VMEM((ys, 2 * EXTRA, chans // 2), F32),
        pltpu.VMEM((2 * xs, slice_rows, chans), BF16),
        pltpu.VMEM(gate_taps.shape, F32),
        pltpu.VMEM(value_featurizer_weights.shape, F32),
        pltpu.SemaphoreType.DMA((4,)),
        pltpu.SemaphoreType.DMA((4,)),
        pltpu.SemaphoreType.DMA((2,)),
        pltpu.SemaphoreType.DMA((2,)),
        pltpu.SemaphoreType.DMA((2,)),
        pltpu.SemaphoreType.DMA((2,)),
        pltpu.SemaphoreType.DMA((8,)),
        pltpu.SemaphoreType.DMA((7,)),
        pltpu.SemaphoreType.DMA((7,)),
    ]
    results = pl.pallas_call(
        functools.partial(kernel, (nctx, ntp, xs, ys, taps, scale)),
        out_shape=(
            jax.ShapeDtypeStruct((tokens, width), BF16),
            jax.ShapeDtypeStruct((taps, width), F32),
            jax.ShapeDtypeStruct(gate_taps.shape, F32),
            jax.ShapeDtypeStruct(value_featurizer_weights.shape, F32),
        ),
        in_specs=[hbm] * 9,
        out_specs=(vmem, vmem, vmem, vmem),
        scratch_shapes=scratch,
        compiler_params=pltpu.CompilerParams(
            collective_id=0, has_side_effects=True, vmem_limit_bytes=55_900_000
        ),
    )(
        out_grad, saved_input, explicit_filter_weights, gate_taps, value_featurizer_weights,
        *matrices,
    )
    return pl.pallas_call(
        write_out,
        out_shape=[jax.ShapeDtypeStruct(r.shape, r.dtype) for r in results],
        in_specs=[vmem] * 4,
        out_specs=[hbm] * 4,
        scratch_shapes=[pltpu.SemaphoreType.DMA((4,))],
        compiler_params=pltpu.CompilerParams(vmem_limit_bytes=2**20),
    )(*results)


def solution(mesh):
    placed = (
        P(("ctx", "tp"), None),
        P(("ctx", "tp"), None),
        P(None, "tp"),
        P(None, "tp"),
        P(None, "tp"),
    )
    return jax.shard_map(
        functools.partial(shards, mesh),
        mesh=mesh,
        in_specs=placed,
        out_specs=(P("ctx", "tp"), P(None, "tp"), P(None, "tp"), P(None, "tp")),
        check_vma=False,
    )
```

```python
import functools
import math

import jax
import jax.numpy as jnp
import ml_dtypes
import numpy as np
from jax import lax
from jax.experimental import pallas as pl
from jax.experimental.pallas import tpu as pltpu
from jax.sharding import PartitionSpec as P

MESH = pl.DeviceIdType.MESH
F32 = jnp.float32
BF16 = jnp.bfloat16
EXTRA = 8


def two_parts(matrix):
    high = matrix.astype(ml_dtypes.bfloat16)
    low = (matrix - high.astype(np.float64)).astype(ml_dtypes.bfloat16)
    return high, low


def transforms(length):
    odd = 2 * np.arange(length // 2)[:, None] + 1
    steps = (odd * np.arange(length)[None, :]) % (2 * length)
    angle = np.pi * steps / length
    forward = np.concatenate([np.cos(angle), -np.sin(angle)])
    inverse = forward.T * (2.0 / length)
    return two_parts(forward) + two_parts(inverse)


def split(x):
    high = x.astype(BF16)
    return high, (x - high.astype(F32)).astype(BF16)


def dot3(ah, al, xh, xl):
    def dot(a, b):
        return jnp.dot(a, b, preferred_element_type=F32)

    return dot(ah, xh) + dot(ah, xl) + dot(al, xh)


def kernel(
    sizes,
    og, si, h_hbm, gt_hbm, w_hbm, fh_hbm, fl_hbm, ih_hbm, il_hbm,
    ig_out, efg_out, gate_out, value_out,
    ubuf, gbuf, hb, fh, fl, ih, il,
    hs, vs, ds, uf, qb, zb, xh, xl, w1b, dqb, igb, head, head_in,
    uh, part, part_in, ep, ep_in, ext, ext_in, rs, xr, xe, yr, ye, ag, gt_ref, w_ref,
    a2a_send, a2a_recv, halo_send, halo_recv, head_send, head_recv,
    const_sem, one_send, one_recv,
):
    nctx, ntp, xs, ys, taps, scale = sizes
    rows, width = og.shape[0], og.shape[1] // ntp
    tokens = rows * ntp
    chans = width // 2
    halo = ubuf.shape[1] - tokens
    length = tokens + taps
    half_len = length // 2
    slice_rows = taps // xs
    ctx, tp = lax.axis_index("ctx"), lax.axis_index("tp")
    core = lax.rem(ctx, 2)
    x = lax.rem(ctx // 2, xs)
    ylo = ctx // (2 * xs)
    deep = ntp // 2
    tp_far = sorted(range(deep), key=lambda d: -min(d, deep - d))
    tp_order = [(far, d) for d in tp_far for far in (1, 0) if far or d]
    x_order = sorted(range(1, xs), key=lambda d: -min(d, xs - d))
    row_order = [(d, c) for d in x_order for c in range(2)] + [(0, 1)]

    def remote(src, dst, send, recv, to_ctx, to_tp):
        return pltpu.make_async_remote_copy(
            src_ref=src, dst_ref=dst, send_sem=send, recv_sem=recv,
            device_id=(to_ctx, to_tp), device_id_type=MESH,
        )

    def finish(ref, sem):
        pltpu.make_async_copy(ref, ref, sem).wait()

    def offset(k):
        half = (1 - core) if k == 0 else core
        return pl.multiple_of(half * chans, chans)

    def tp_peer(step):
        far, d = step
        return lax.rem(tp // deep + far, 2) * deep + lax.rem(lax.rem(tp, deep) + d, deep)

    def x_peer(d):
        return lax.rem(x + d, xs)

    def row_peer(step):
        d, c = step
        return (ylo * xs + x_peer(d)) * 2 + lax.rem(core + c, 2)

    def x_ctx(other):
        return (ylo * xs + other) * 2 + core

    def y_ctx(i):
        return (lax.rem(ylo + i, ys) * xs + x) * 2 + core

    barrier = pltpu.get_barrier_semaphore()

    def greet(to_ctx, to_tp):
        pl.semaphore_signal(barrier, inc=1, device_id=(to_ctx, to_tp), device_id_type=MESH)

    for step in tp_order:
        greet(ctx, tp_peer(step))
    for step in row_order:
        greet(row_peer(step), tp)
    for i in range(1, ys):
        greet(y_ctx(i), tp)

    @pl.when(ctx > 0)
    def _():
        greet(ctx - 1, tp)

    @pl.when(ctx < nctx - 1)
    def _():
        greet(ctx + 1, tp)

    constants = [
        pltpu.make_async_copy(src, dst, const_sem.at[i])
        for i, (src, dst) in enumerate(
            [(fh_hbm, fh), (fl_hbm, fl), (ih_hbm, ih), (il_hbm, il), (gt_hbm, gt_ref), (w_hbm, w_ref)]
            + [(h_hbm.at[:, pl.ds(offset(k), chans)], hb.at[k]) for k in range(2)]
        )
    ]
    for copy in constants:
        copy.start()

    @pl.when(ctx == 0)
    def _():
        ubuf[:, 0:halo, :] = jnp.zeros((2, halo, chans), BF16)

    @pl.when(ctx == nctx - 1)
    def _():
        head_in[...] = jnp.zeros(head_in.shape, BF16)

    greeted = ntp - 1 + 2 * xs - 1 + ys - 1
    greeted = greeted + jnp.where(ctx > 0, 1, 0) + jnp.where(ctx < nctx - 1, 1, 0)
    pl.semaphore_wait(barrier, greeted)

    def exchange(src, dst, base, k, sem):
        def columns(who):
            return src.at[:, pl.ds(pl.multiple_of(who * width + offset(k), chans), chans)]

        place = dst.at[k, pl.ds(pl.multiple_of(base + tp * rows, 16), rows), :]
        for step in tp_order:
            to = tp_peer(step)
            remote(columns(to), place, a2a_send.at[sem], a2a_recv.at[sem], ctx, to).start()
        pltpu.make_async_copy(columns(tp), place, a2a_recv.at[sem]).start()

    exchange(si, ubuf, halo, 0, 0)
    exchange(si, ubuf, halo, 1, 1)
    exchange(og, gbuf, 0, 0, 2)
    exchange(og, gbuf, 0, 1, 3)

    for copy in constants:
        copy.wait()
    for k in range(2):
        th, tl = split(hb[k])
        hs[k] = dot3(fh[:, 0:taps], fl[:, 0:taps], th, tl)
    w1b[:, 0:16, :] = jnp.zeros((2, 16, chans), F32)
    w1b[:, 16 + length : 32 + length, :] = jnp.zeros((2, 16, chans), F32)
    dqb[:, 0:16, :] = jnp.zeros((2, 16, chans), F32)
    dqb[:, 16 + tokens : 32 + tokens, :] = jnp.zeros((2, 16, chans), F32)

    def taps_of(ref, k):
        block = ref[:, pl.ds(offset(k), chans)]
        return [block[i : i + 1] for i in range(3)]

    def halo_copy(k):
        return remote(
            ubuf.at[k, pl.ds(tokens, halo), :], ubuf.at[1 - k, pl.ds(0, halo), :],
            halo_send.at[k], halo_recv.at[1 - k], ctx + 1, tp,
        )

    def spectrum_product(a, a_k, b, b_k, sign):
        for r in range(0, half_len, 32):
            ar, ai = a[a_k, r : r + 32], a[a_k, half_len + r : half_len + r + 32]
            br, bi = b[b_k, r : r + 32], b[b_k, half_len + r : half_len + r + 32]
            if sign > 0:
                re, im = ar * br - ai * bi, ar * bi + ai * br
            else:
                re, im = ar * br + ai * bi, ar * bi - ai * br
            xh[r : r + 32], xl[r : r + 32] = split(re)
            xh[half_len + r : half_len + r + 32], xl[half_len + r : half_len + r + 32] = split(im)

    def delayed(ref, k, r, count):
        first = halo - taps + r
        return [ref[k, first - i : first - i + count] for i in range(3)]

    def mixed(weights, signals):
        return weights[0] * signals[0] + weights[1] * signals[1] + weights[2] * signals[2]

    def own_spectrum(k):
        finish(ubuf.at[k, pl.ds(halo, tokens), :], a2a_recv.at[k])

        @pl.when(ctx < nctx - 1)
        def _():
            halo_copy(k).start()

        wv, wg = taps_of(w_ref, k), taps_of(gt_ref, k)
        for r in range(halo, halo + tokens, 32):
            uf[k, r : r + 32] = ubuf[k, r : r + 32].astype(F32)
        for r in range(taps, length, 32):
            u = delayed(uf, k, r, 32)
            xh[r : r + 32], xl[r : r + 32] = split(mixed(wv, u))
            qb[k, r - taps : r - taps + 32] = mixed(wg, u)
        vs[k] = dot3(fh[:, taps:], fl[:, taps:], xh[taps:, :], xl[taps:, :])

    def halo_spectrum(k):
        @pl.when(ctx > 0)
        def _():
            finish(ubuf.at[k, pl.ds(0, halo), :], halo_recv.at[k])

        wv, wg = taps_of(w_ref, k), taps_of(gt_ref, k)
        for r in range(0, halo, 16):
            block = ubuf[k, r : r + 16].astype(F32)
            uf[k, r : r + 16] = block
            uh[0, r : r + 16] = block
        for r in range(0, taps + 16, 16):
            xh[r : r + 16], xl[r : r + 16] = split(mixed(wv, delayed(uh, 0, r, 16)))
        blank = jnp.zeros((tokens - taps - 16, chans), BF16)
        xh[taps + 16 : tokens] = blank
        xl[taps + 16 : tokens] = blank
        qb[k, 0:16] = mixed(wg, delayed(uf, k, taps, 16))
        vs[k] += dot3(fh[:, :tokens], fl[:, :tokens], xh[:tokens, :], xl[:tokens, :])
        spectrum_product(hs, k, vs, k, 1)
        zb[k] = dot3(ih[taps:, :], il[taps:, :], xh[...], xl[...])

    def fold(values):
        return jnp.sum(values.reshape(values.shape[0] // 8, 8, chans), axis=0)

    def input_gradient(k):
        wv, wg = taps_of(w_ref, k), taps_of(gt_ref, k)
        for r in range(0, halo + tokens, 16):
            a = [w1b[k, r + i : r + i + 16] for i in range(3)]
            total = wv[0] * a[0] + wv[1] * a[1] + wv[2] * a[2]
            first = r - halo
            if first >= -16:
                d = [dqb[k, 16 + first + i : 32 + first + i] for i in range(3)]
                total = total + wg[0] * d[0] + wg[1] * d[1] + wg[2] * d[2]
            if first < 0:
                head[k, r : r + 16] = total.astype(BF16)
            else:
                igb[k, first : first + 16] = total

        @pl.when(ctx > 0)
        def _():
            remote(
                head.at[k], head_in.at[1 - k], head_send.at[k], head_recv.at[1 - k], ctx - 1, tp
            ).start()

    partner = ctx + 1 - 2 * core

    def filter_part(k):
        finish(gbuf.at[k], a2a_recv.at[2 + k])
        for r in range(0, tokens, 32):
            g = gbuf[k, r : r + 32].astype(F32)
            xh[taps + r : taps + r + 32], xl[taps + r : taps + r + 32] = split(
                g * qb[k, r : r + 32]
            )
            dqb[k, 16 + r : 48 + r] = g * zb[k, r : r + 32]
        ds[k] = dot3(fh[:, taps:], fl[:, taps:], xh[taps:, :], xl[taps:, :])
        spectrum_product(vs, k, ds, k, -1)
        part[k] = dot3(ih[0:taps, :], il[0:taps, :], xh[...], xl[...]) * scale

    def extra_part(k):
        spectrum_product(hs, k, ds, k, -1)
        w1b[k, 16 : 16 + length] = dot3(ih[...], il[...], xh[...], xl[...])
        sums = [jnp.zeros((8, chans), F32) for _ in range(6)]
        for r in range(0, length, 32):
            u = delayed(uf, k, r, 32)
            w1 = w1b[k, 16 + r : 48 + r]
            if r >= taps:
                dq = dqb[k, 16 + r - taps : 48 + r - taps]
                sums[:3] = [s + fold(dq * d) for s, d in zip(sums[:3], u)]
            sums[3:] = [s + fold(w1 * d) for s, d in zip(sums[3:], u)]
        for i, s in enumerate(sums):
            total = jnp.sum(s, axis=0, keepdims=True) * scale
            for lane in range(2):
                ep[k, 8 * lane + i : 8 * lane + i + 1] = total[
                    :, lane * (chans // 2) : (lane + 1) * (chans // 2)
                ]

    ep[...] = jnp.zeros(ep.shape, F32)
    uf[:, halo - 16 : halo] = jnp.zeros((2, 16, chans), F32)
    uh[0, halo : halo + 16] = jnp.zeros((16, chans), F32)
    own_spectrum(0)
    own_spectrum(1)
    halo_spectrum(0)
    filter_part(0)
    remote(part.at[0], part_in, one_send.at[0], one_recv.at[0], partner, tp).start()
    halo_spectrum(1)
    extra_part(0)
    remote(ep.at[0], ep_in, one_send.at[7], one_recv.at[7], partner, tp).start()
    filter_part(1)
    finish(part_in, one_recv.at[0])
    for s in range(xs):
        rows_of = slice(s * slice_rows, (s + 1) * slice_rows)
        rs[s] = (part[1, rows_of] + part_in[rows_of]).astype(BF16)
    for d in x_order:
        to = x_peer(d)
        remote(rs.at[to], xr.at[x], one_send.at[1], one_recv.at[1], x_ctx(to), tp).start()
    xr[x] = rs[x]
    extra_part(1)
    finish(ep_in, one_recv.at[7])
    xe[x] = (ep[1] + ep_in[...]).astype(BF16)
    for d in x_order:
        remote(
            xe.at[x], xe.at[x], one_send.at[4], one_recv.at[4], x_ctx(x_peer(d)), tp
        ).start()
    input_gradient(0)
    input_gradient(1)
    finish(xr.at[pl.ds(0, xs - 1)], one_recv.at[1])
    total = xr[0].astype(F32)
    for s in range(1, xs):
        total = total + xr[s].astype(F32)
    yr[ylo] = total
    for i in range(1, ys):
        remote(
            yr.at[ylo], yr.at[ylo], one_send.at[2], one_recv.at[2], y_ctx(i), tp
        ).start()
    finish(xe.at[pl.ds(0, xs - 1)], one_recv.at[4])
    total = xe[0].astype(F32)
    for s in range(1, xs):
        total = total + xe[s].astype(F32)
    ye[ylo] = total
    for i in range(1, ys):
        remote(
            ye.at[ylo], ye.at[ylo], one_send.at[5], one_recv.at[5], y_ctx(i), tp
        ).start()

    @pl.when(ctx < nctx - 1)
    def _():
        for k in range(2):
            finish(head_in.at[k], head_recv.at[k])

    for k in range(2):
        for r in range(0, tokens, 16):
            block = igb[k, r : r + 16]
            late = r - (tokens - halo)
            if late >= 0:
                block = block + head_in[k, late : late + 16].astype(F32)
            ig_out[r : r + 16, pl.ds(offset(k), chans)] = block.astype(BF16)

    finish(yr.at[pl.ds(0, ys - 1)], one_recv.at[2])
    total = yr[0]
    for s in range(1, ys):
        total = total + yr[s]
    slot = core * xs + x
    ag[slot] = total.astype(BF16)
    for step in row_order:
        remote(
            ag.at[slot], ag.at[slot], one_send.at[3], one_recv.at[3], row_peer(step), tp
        ).start()
    finish(ye.at[pl.ds(0, ys - 1)], one_recv.at[5])
    total = ye[0]
    for s in range(1, ys):
        total = total + ye[s]
    ext[...] = total
    remote(ext, ext_in, one_send.at[6], one_recv.at[6], partner, tp).start()

    def put_extra(source, k):
        for lane in range(2):
            place = pl.ds(pl.multiple_of(offset(k) + lane * (chans // 2), chans // 2), chans // 2)
            gate_out[:, place] = source[8 * lane : 8 * lane + 3]
            value_out[:, place] = source[8 * lane + 3 : 8 * lane + 6]

    put_extra(ext, 1)
    finish(ext_in, one_recv.at[6])
    put_extra(ext_in, 0)
    finish(ag.at[pl.ds(0, 2 * xs - 1)], one_recv.at[3])
    for half in range(2):
        for s in range(xs):
            efg_out[
                s * slice_rows : (s + 1) * slice_rows, half * chans : (half + 1) * chans
            ] = ag[half * xs + s].astype(F32)

    for k in range(2):
        finish(ubuf.at[k, pl.ds(0, rows * (ntp - 1)), :], a2a_send.at[k])
        finish(gbuf.at[k, pl.ds(0, rows * (ntp - 1)), :], a2a_send.at[2 + k])

        @pl.when(ctx < nctx - 1)
        def _(k=k):
            finish(ubuf.at[k, pl.ds(0, halo), :], halo_send.at[k])

        @pl.when(ctx > 0)
        def _(k=k):
            finish(head.at[k], head_send.at[k])

    finish(rs.at[pl.ds(0, xs - 1)], one_send.at[1])
    finish(yr.at[pl.ds(0, ys - 1)], one_send.at[2])
    finish(ag.at[pl.ds(0, 2 * xs - 1)], one_send.at[3])
    finish(xe.at[pl.ds(0, xs - 1)], one_send.at[4])
    finish(ye.at[pl.ds(0, ys - 1)], one_send.at[5])
    finish(ext, one_send.at[6])
    finish(part_in, one_send.at[0])
    finish(ep_in, one_send.at[7])


def write_out(*refs):
    copies = [
        pltpu.make_async_copy(refs[i], refs[4 + i], refs[8].at[i]) for i in range(4)
    ]
    for copy in copies:
        copy.start()
    for copy in copies:
        copy.wait()


def shards(mesh, out_grad, saved_input, explicit_filter_weights, gate_taps, value_featurizer_weights):
    nctx, ntp = mesh.shape["ctx"], mesh.shape["tp"]
    rows, channels = out_grad.shape
    width = channels // ntp
    tokens = rows * ntp
    taps = explicit_filter_weights.shape[0]
    xs = 8 if nctx >= 64 else 2
    ys = nctx // (2 * xs)
    chans = width // 2
    halo = -(-(taps + gate_taps.shape[0] - 2) // 16) * 16
    length = tokens + taps
    slice_rows = taps // xs
    scale = np.float32(1.0 / math.sqrt(tokens * nctx))
    matrices = [jnp.asarray(m) for m in transforms(length)]
    hbm = pl.BlockSpec(memory_space=pltpu.HBM)
    vmem = pl.BlockSpec(memory_space=pltpu.VMEM)
    scratch = [
        pltpu.VMEM((2, halo + tokens, chans), BF16),
        pltpu.VMEM((2, tokens, chans), BF16),
        pltpu.VMEM((2, taps, chans), F32),
        *[pltpu.VMEM((length, length), BF16) for _ in range(4)],
        pltpu.VMEM((2, length, chans), F32),
        pltpu.VMEM((2, length, chans), F32),
        pltpu.VMEM((2, length, chans), F32),
        pltpu.VMEM((2, halo + tokens, chans), F32),
        pltpu.VMEM((2, tokens, chans), F32),
        pltpu.VMEM((2, tokens, chans), F32),
        pltpu.VMEM((length, chans), BF16),
        pltpu.VMEM((length, chans), BF16),
        pltpu.VMEM((2, length + 32, chans), F32),
        pltpu.VMEM((2, tokens + 32, chans), F32),
        pltpu.VMEM((2, tokens, chans), F32),
        pltpu.VMEM((2, halo, chans), BF16),
        pltpu.VMEM((2, halo, chans), BF16),
        pltpu.VMEM((1, halo + 16, chans), F32),
        pltpu.VMEM((2, taps, chans), F32),
        pltpu.VMEM((taps, chans), F32),
        pltpu.VMEM((2, 2 * EXTRA, chans // 2), F32),
        pltpu.VMEM((2 * EXTRA, chans // 2), F32),
        pltpu.VMEM((2 * EXTRA, chans // 2), F32),
        pltpu.VMEM((2 * EXTRA, chans // 2), F32),
        pltpu.VMEM((xs, slice_rows, chans), BF16),
        pltpu.VMEM((xs, slice_rows, chans), BF16),
        pltpu.VMEM((xs, 2 * EXTRA, chans // 2), BF16),
        pltpu.VMEM((ys, slice_rows, chans), F32),
        pltpu.VMEM((ys, 2 * EXTRA, chans // 2), F32),
        pltpu.VMEM((2 * xs, slice_rows, chans), BF16),
        pltpu.VMEM(gate_taps.shape, F32),
        pltpu.VMEM(value_featurizer_weights.shape, F32),
        pltpu.SemaphoreType.DMA((4,)),
        pltpu.SemaphoreType.DMA((4,)),
        pltpu.SemaphoreType.DMA((2,)),
        pltpu.SemaphoreType.DMA((2,)),
        pltpu.SemaphoreType.DMA((2,)),
        pltpu.SemaphoreType.DMA((2,)),
        pltpu.SemaphoreType.DMA((8,)),
        pltpu.SemaphoreType.DMA((8,)),
        pltpu.SemaphoreType.DMA((8,)),
    ]
    results = pl.pallas_call(
        functools.partial(kernel, (nctx, ntp, xs, ys, taps, scale)),
        out_shape=(
            jax.ShapeDtypeStruct((tokens, width), BF16),
            jax.ShapeDtypeStruct((taps, width), F32),
            jax.ShapeDtypeStruct(gate_taps.shape, F32),
            jax.ShapeDtypeStruct(value_featurizer_weights.shape, F32),
        ),
        in_specs=[hbm] * 9,
        out_specs=(vmem, vmem, vmem, vmem),
        scratch_shapes=scratch,
        compiler_params=pltpu.CompilerParams(
            collective_id=0, has_side_effects=True, vmem_limit_bytes=55_900_000
        ),
    )(
        out_grad, saved_input, explicit_filter_weights, gate_taps, value_featurizer_weights,
        *matrices,
    )
    return pl.pallas_call(
        write_out,
        out_shape=[jax.ShapeDtypeStruct(r.shape, r.dtype) for r in results],
        in_specs=[vmem] * 4,
        out_specs=[hbm] * 4,
        scratch_shapes=[pltpu.SemaphoreType.DMA((4,))],
        compiler_params=pltpu.CompilerParams(vmem_limit_bytes=2**20),
    )(*results)


def solution(mesh):
    placed = (
        P(("ctx", "tp"), None),
        P(("ctx", "tp"), None),
        P(None, "tp"),
        P(None, "tp"),
        P(None, "tp"),
    )
    return jax.shard_map(
        functools.partial(shards, mesh),
        mesh=mesh,
        in_specs=placed,
        out_specs=(P("ctx", "tp"), P(None, "tp"), P(None, "tp"), P(None, "tp")),
        check_vma=False,
    )
```

```python
import functools
import math

import jax
import jax.numpy as jnp
import ml_dtypes
import numpy as np
from jax import lax
from jax.experimental import pallas as pl
from jax.experimental.pallas import tpu as pltpu
from jax.sharding import PartitionSpec as P

MESH = pl.DeviceIdType.MESH
F32 = jnp.float32
BF16 = jnp.bfloat16
EXTRA = 8


def two_parts(matrix):
    high = matrix.astype(ml_dtypes.bfloat16)
    low = (matrix - high.astype(np.float64)).astype(ml_dtypes.bfloat16)
    return high, low


def transforms(length):
    odd = 2 * np.arange(length // 2)[:, None] + 1
    steps = (odd * np.arange(length)[None, :]) % (2 * length)
    angle = np.pi * steps / length
    forward = np.concatenate([np.cos(angle), -np.sin(angle)])
    inverse = forward.T * (2.0 / length)
    return two_parts(forward) + two_parts(inverse)


def split(x):
    high = x.astype(BF16)
    return high, (x - high.astype(F32)).astype(BF16)


def dot3(ah, al, xh, xl):
    def dot(a, b):
        return jnp.dot(a, b, preferred_element_type=F32)

    return dot(ah, xh) + dot(ah, xl) + dot(al, xh)


def kernel(
    sizes,
    og, si, h_hbm, gt_hbm, w_hbm, fh_hbm, fl_hbm, ih_hbm, il_hbm,
    ig_out, efg_out, gate_out, value_out,
    ubuf, gbuf, hb, fh, fl, ih, il,
    hs, vs, ds, uf, qb, zb, xh, xl, w1b, dqb, igb, head, head_in,
    uh, part, part_in, ep, ep_in, ext, ext_in, rs, xr, xe, yr, ye, ag, gt_ref, w_ref,
    a2a_send, a2a_recv, halo_send, halo_recv, head_send, head_recv,
    const_sem, one_send, one_recv,
):
    nctx, ntp, xs, ys, taps, scale = sizes
    rows, width = og.shape[0], og.shape[1] // ntp
    tokens = rows * ntp
    chans = width // 2
    halo = ubuf.shape[1] - tokens
    length = tokens + taps
    half_len = length // 2
    slice_rows = taps // xs
    ctx, tp = lax.axis_index("ctx"), lax.axis_index("tp")
    core = lax.rem(ctx, 2)
    x = lax.rem(ctx // 2, xs)
    ylo = ctx // (2 * xs)
    deep = ntp // 2
    tp_far = sorted(range(deep), key=lambda d: -min(d, deep - d))
    across, along = [(1, d) for d in tp_far], [(0, d) for d in tp_far if d]
    tp_order = []
    while across or along:
        tp_order += across[:2] + along[:1]
        across, along = across[2:], along[1:]
    x_order = sorted(range(1, xs), key=lambda d: -min(d, xs - d))
    row_order = [(d, c) for d in x_order for c in range(2)] + [(0, 1)]

    def remote(src, dst, send, recv, to_ctx, to_tp):
        return pltpu.make_async_remote_copy(
            src_ref=src, dst_ref=dst, send_sem=send, recv_sem=recv,
            device_id=(to_ctx, to_tp), device_id_type=MESH,
        )

    def finish(ref, sem):
        pltpu.make_async_copy(ref, ref, sem).wait()

    def offset(k):
        half = (1 - core) if k == 0 else core
        return pl.multiple_of(half * chans, chans)

    def tp_peer(step):
        far, d = step
        return lax.rem(tp // deep + far, 2) * deep + lax.rem(lax.rem(tp, deep) + d, deep)

    def x_peer(d):
        return lax.rem(x + d, xs)

    def row_peer(step):
        d, c = step
        return (ylo * xs + x_peer(d)) * 2 + lax.rem(core + c, 2)

    def x_ctx(other):
        return (ylo * xs + other) * 2 + core

    def y_ctx(i):
        low = ylo < ys // 2
        pair = [jnp.where(low, ys - 1, 0), jnp.where(low, ys - 2, 1)]
        other = ylo + 1 - 2 * lax.rem(ylo, 2)
        to = [pair[0], pair[1], other][i - 1] if ys == 4 else lax.rem(ylo + i, ys)
        return (to * xs + x) * 2 + core

    barrier = pltpu.get_barrier_semaphore()

    def greet(to_ctx, to_tp):
        pl.semaphore_signal(barrier, inc=1, device_id=(to_ctx, to_tp), device_id_type=MESH)

    for step in tp_order:
        greet(ctx, tp_peer(step))
    for step in row_order:
        greet(row_peer(step), tp)
    for i in range(1, ys):
        greet(y_ctx(i), tp)

    @pl.when(ctx > 0)
    def _():
        greet(ctx - 1, tp)

    @pl.when(ctx < nctx - 1)
    def _():
        greet(ctx + 1, tp)

    constants = [
        pltpu.make_async_copy(src, dst, const_sem.at[i])
        for i, (src, dst) in enumerate(
            [(fh_hbm, fh), (fl_hbm, fl), (ih_hbm, ih), (il_hbm, il), (gt_hbm, gt_ref), (w_hbm, w_ref)]
            + [(h_hbm.at[:, pl.ds(offset(k), chans)], hb.at[k]) for k in range(2)]
        )
    ]
    for copy in constants:
        copy.start()

    @pl.when(ctx == 0)
    def _():
        ubuf[:, 0:halo, :] = jnp.zeros((2, halo, chans), BF16)

    @pl.when(ctx == nctx - 1)
    def _():
        head_in[...] = jnp.zeros(head_in.shape, BF16)

    greeted = ntp - 1 + 2 * xs - 1 + ys - 1
    greeted = greeted + jnp.where(ctx > 0, 1, 0) + jnp.where(ctx < nctx - 1, 1, 0)
    pl.semaphore_wait(barrier, greeted)

    def exchange(src, dst, base, k, sem):
        def columns(who):
            return src.at[:, pl.ds(pl.multiple_of(who * width + offset(k), chans), chans)]

        place = dst.at[k, pl.ds(pl.multiple_of(base + tp * rows, 16), rows), :]
        for step in tp_order:
            to = tp_peer(step)
            remote(columns(to), place, a2a_send.at[sem], a2a_recv.at[sem], ctx, to).start()
        pltpu.make_async_copy(columns(tp), place, a2a_recv.at[sem]).start()

    exchange(si, ubuf, halo, 0, 0)
    exchange(si, ubuf, halo, 1, 1)
    exchange(og, gbuf, 0, 0, 2)
    exchange(og, gbuf, 0, 1, 3)

    for copy in constants:
        copy.wait()
    for k in range(2):
        th, tl = split(hb[k])
        hs[k] = dot3(fh[:, 0:taps], fl[:, 0:taps], th, tl)
    w1b[:, 0:16, :] = jnp.zeros((2, 16, chans), F32)
    w1b[:, 16 + length : 32 + length, :] = jnp.zeros((2, 16, chans), F32)
    dqb[:, 0:16, :] = jnp.zeros((2, 16, chans), F32)
    dqb[:, 16 + tokens : 32 + tokens, :] = jnp.zeros((2, 16, chans), F32)

    def taps_of(ref, k):
        block = ref[:, pl.ds(offset(k), chans)]
        return [block[i : i + 1] for i in range(3)]

    def halo_copy(k):
        return remote(
            ubuf.at[k, pl.ds(tokens, halo), :], ubuf.at[1 - k, pl.ds(0, halo), :],
            halo_send.at[k], halo_recv.at[1 - k], ctx + 1, tp,
        )

    def spectrum_product(a, a_k, b, b_k, sign):
        for r in range(0, half_len, 32):
            ar, ai = a[a_k, r : r + 32], a[a_k, half_len + r : half_len + r + 32]
            br, bi = b[b_k, r : r + 32], b[b_k, half_len + r : half_len + r + 32]
            if sign > 0:
                re, im = ar * br - ai * bi, ar * bi + ai * br
            else:
                re, im = ar * br + ai * bi, ar * bi - ai * br
            xh[r : r + 32], xl[r : r + 32] = split(re)
            xh[half_len + r : half_len + r + 32], xl[half_len + r : half_len + r + 32] = split(im)

    def delayed(ref, k, r, count):
        first = halo - taps + r
        return [ref[k, first - i : first - i + count] for i in range(3)]

    def mixed(weights, signals):
        return weights[0] * signals[0] + weights[1] * signals[1] + weights[2] * signals[2]

    def own_spectrum(k):
        finish(ubuf.at[k, pl.ds(halo, tokens), :], a2a_recv.at[k])

        @pl.when(ctx < nctx - 1)
        def _():
            halo_copy(k).start()

        wv, wg = taps_of(w_ref, k), taps_of(gt_ref, k)
        for r in range(halo, halo + tokens, 32):
            uf[k, r : r + 32] = ubuf[k, r : r + 32].astype(F32)
        for r in range(taps, length, 32):
            u = delayed(uf, k, r, 32)
            xh[r : r + 32], xl[r : r + 32] = split(mixed(wv, u))
            qb[k, r - taps : r - taps + 32] = mixed(wg, u)
        vs[k] = dot3(fh[:, taps:], fl[:, taps:], xh[taps:, :], xl[taps:, :])

    def halo_spectrum(k):
        @pl.when(ctx > 0)
        def _():
            finish(ubuf.at[k, pl.ds(0, halo), :], halo_recv.at[k])

        wv, wg = taps_of(w_ref, k), taps_of(gt_ref, k)
        for r in range(0, halo, 16):
            block = ubuf[k, r : r + 16].astype(F32)
            uf[k, r : r + 16] = block
            uh[0, r : r + 16] = block
        for r in range(0, taps + 16, 16):
            xh[r : r + 16], xl[r : r + 16] = split(mixed(wv, delayed(uh, 0, r, 16)))
        blank = jnp.zeros((tokens - taps - 16, chans), BF16)
        xh[taps + 16 : tokens] = blank
        xl[taps + 16 : tokens] = blank
        qb[k, 0:16] = mixed(wg, delayed(uf, k, taps, 16))
        vs[k] += dot3(fh[:, :tokens], fl[:, :tokens], xh[:tokens, :], xl[:tokens, :])
        spectrum_product(hs, k, vs, k, 1)
        zb[k] = dot3(ih[taps:, :], il[taps:, :], xh[...], xl[...])

    def fold(values):
        return jnp.sum(values.reshape(values.shape[0] // 8, 8, chans), axis=0)

    def input_gradient(k):
        wv, wg = taps_of(w_ref, k), taps_of(gt_ref, k)
        for r in range(0, halo + tokens, 16):
            a = [w1b[k, r + i : r + i + 16] for i in range(3)]
            total = wv[0] * a[0] + wv[1] * a[1] + wv[2] * a[2]
            first = r - halo
            if first >= -16:
                d = [dqb[k, 16 + first + i : 32 + first + i] for i in range(3)]
                total = total + wg[0] * d[0] + wg[1] * d[1] + wg[2] * d[2]
            if first < 0:
                head[k, r : r + 16] = total.astype(BF16)
            else:
                igb[k, first : first + 16] = total

        @pl.when(ctx > 0)
        def _():
            remote(
                head.at[k], head_in.at[1 - k], head_send.at[k], head_recv.at[1 - k], ctx - 1, tp
            ).start()

    partner = ctx + 1 - 2 * core

    def filter_part(k):
        finish(gbuf.at[k], a2a_recv.at[2 + k])
        for r in range(0, tokens, 32):
            g = gbuf[k, r : r + 32].astype(F32)
            xh[taps + r : taps + r + 32], xl[taps + r : taps + r + 32] = split(
                g * qb[k, r : r + 32]
            )
            dqb[k, 16 + r : 48 + r] = g * zb[k, r : r + 32]
        ds[k] = dot3(fh[:, taps:], fl[:, taps:], xh[taps:, :], xl[taps:, :])
        spectrum_product(vs, k, ds, k, -1)
        part[k] = dot3(ih[0:taps, :], il[0:taps, :], xh[...], xl[...]) * scale

    def extra_part(k):
        spectrum_product(hs, k, ds, k, -1)
        w1b[k, 16 : 16 + length] = dot3(ih[...], il[...], xh[...], xl[...])
        sums = [jnp.zeros((8, chans), F32) for _ in range(6)]
        for r in range(0, length, 32):
            u = delayed(uf, k, r, 32)
            w1 = w1b[k, 16 + r : 48 + r]
            if r >= taps:
                dq = dqb[k, 16 + r - taps : 48 + r - taps]
                sums[:3] = [s + fold(dq * d) for s, d in zip(sums[:3], u)]
            sums[3:] = [s + fold(w1 * d) for s, d in zip(sums[3:], u)]
        for i, s in enumerate(sums):
            total = jnp.sum(s, axis=0, keepdims=True) * scale
            for lane in range(2):
                ep[k, 8 * lane + i : 8 * lane + i + 1] = total[
                    :, lane * (chans // 2) : (lane + 1) * (chans // 2)
                ]

    ep[...] = jnp.zeros(ep.shape, F32)
    uf[:, halo - 16 : halo] = jnp.zeros((2, 16, chans), F32)
    uh[0, halo : halo + 16] = jnp.zeros((16, chans), F32)
    own_spectrum(0)
    own_spectrum(1)
    halo_spectrum(0)
    filter_part(0)
    remote(part.at[0], part_in, one_send.at[0], one_recv.at[0], partner, tp).start()
    halo_spectrum(1)
    filter_part(1)
    finish(part_in, one_recv.at[0])
    for s in range(xs):
        rows_of = slice(s * slice_rows, (s + 1) * slice_rows)
        rs[s] = (part[1, rows_of] + part_in[rows_of]).astype(BF16)
    for d in x_order:
        to = x_peer(d)
        remote(rs.at[to], xr.at[x], one_send.at[1], one_recv.at[1], x_ctx(to), tp).start()
    xr[x] = rs[x]
    extra_part(0)
    remote(ep.at[0], ep_in, one_send.at[7], one_recv.at[7], partner, tp).start()
    extra_part(1)
    finish(ep_in, one_recv.at[7])
    xe[x] = (ep[1] + ep_in[...]).astype(BF16)
    for d in x_order:
        remote(
            xe.at[x], xe.at[x], one_send.at[4], one_recv.at[4], x_ctx(x_peer(d)), tp
        ).start()
    input_gradient(0)
    input_gradient(1)
    finish(xr.at[pl.ds(0, xs - 1)], one_recv.at[1])
    total = xr[0].astype(F32)
    for s in range(1, xs):
        total = total + xr[s].astype(F32)
    yr[ylo] = total
    for i in range(1, ys):
        remote(
            yr.at[ylo], yr.at[ylo], one_send.at[2], one_recv.at[2], y_ctx(i), tp
        ).start()
    finish(xe.at[pl.ds(0, xs - 1)], one_recv.at[4])
    total = xe[0].astype(F32)
    for s in range(1, xs):
        total = total + xe[s].astype(F32)
    ye[ylo] = total
    for i in range(1, ys):
        remote(
            ye.at[ylo], ye.at[ylo], one_send.at[5], one_recv.at[5], y_ctx(i), tp
        ).start()

    @pl.when(ctx < nctx - 1)
    def _():
        for k in range(2):
            finish(head_in.at[k], head_recv.at[k])

    for k in range(2):
        for r in range(0, tokens, 16):
            block = igb[k, r : r + 16]
            late = r - (tokens - halo)
            if late >= 0:
                block = block + head_in[k, late : late + 16].astype(F32)
            ig_out[r : r + 16, pl.ds(offset(k), chans)] = block.astype(BF16)

    finish(yr.at[pl.ds(0, ys - 1)], one_recv.at[2])
    total = yr[0]
    for s in range(1, ys):
        total = total + yr[s]
    slot = core * xs + x
    ag[slot] = total.astype(BF16)
    for step in row_order:
        remote(
            ag.at[slot], ag.at[slot], one_send.at[3], one_recv.at[3], row_peer(step), tp
        ).start()
    finish(ye.at[pl.ds(0, ys - 1)], one_recv.at[5])
    total = ye[0]
    for s in range(1, ys):
        total = total + ye[s]
    ext[...] = total
    remote(ext, ext_in, one_send.at[6], one_recv.at[6], partner, tp).start()

    def put_extra(source, k):
        for lane in range(2):
            place = pl.ds(pl.multiple_of(offset(k) + lane * (chans // 2), chans // 2), chans // 2)
            gate_out[:, place] = source[8 * lane : 8 * lane + 3]
            value_out[:, place] = source[8 * lane + 3 : 8 * lane + 6]

    put_extra(ext, 1)
    finish(ext_in, one_recv.at[6])
    put_extra(ext_in, 0)
    finish(ag.at[pl.ds(0, 2 * xs - 1)], one_recv.at[3])
    for half in range(2):
        for s in range(xs):
            efg_out[
                s * slice_rows : (s + 1) * slice_rows, half * chans : (half + 1) * chans
            ] = ag[half * xs + s].astype(F32)

    for k in range(2):
        finish(ubuf.at[k, pl.ds(0, rows * (ntp - 1)), :], a2a_send.at[k])
        finish(gbuf.at[k, pl.ds(0, rows * (ntp - 1)), :], a2a_send.at[2 + k])

        @pl.when(ctx < nctx - 1)
        def _(k=k):
            finish(ubuf.at[k, pl.ds(0, halo), :], halo_send.at[k])

        @pl.when(ctx > 0)
        def _(k=k):
            finish(head.at[k], head_send.at[k])

    finish(rs.at[pl.ds(0, xs - 1)], one_send.at[1])
    finish(yr.at[pl.ds(0, ys - 1)], one_send.at[2])
    finish(ag.at[pl.ds(0, 2 * xs - 1)], one_send.at[3])
    finish(xe.at[pl.ds(0, xs - 1)], one_send.at[4])
    finish(ye.at[pl.ds(0, ys - 1)], one_send.at[5])
    finish(ext, one_send.at[6])
    finish(part_in, one_send.at[0])
    finish(ep_in, one_send.at[7])


def write_out(*refs):
    copies = [
        pltpu.make_async_copy(refs[i], refs[4 + i], refs[8].at[i]) for i in range(4)
    ]
    for copy in copies:
        copy.start()
    for copy in copies:
        copy.wait()


def shards(mesh, out_grad, saved_input, explicit_filter_weights, gate_taps, value_featurizer_weights):
    nctx, ntp = mesh.shape["ctx"], mesh.shape["tp"]
    rows, channels = out_grad.shape
    width = channels // ntp
    tokens = rows * ntp
    taps = explicit_filter_weights.shape[0]
    xs = 8 if nctx >= 64 else 2
    ys = nctx // (2 * xs)
    chans = width // 2
    halo = -(-(taps + gate_taps.shape[0] - 2) // 16) * 16
    length = tokens + taps
    slice_rows = taps // xs
    scale = np.float32(1.0 / math.sqrt(tokens * nctx))
    matrices = [jnp.asarray(m) for m in transforms(length)]
    hbm = pl.BlockSpec(memory_space=pltpu.HBM)
    vmem = pl.BlockSpec(memory_space=pltpu.VMEM)
    gate_taps = pltpu.with_memory_space_constraint(gate_taps, pltpu.HBM)
    value_featurizer_weights = pltpu.with_memory_space_constraint(value_featurizer_weights, pltpu.HBM)
    scratch = [
        pltpu.VMEM((2, halo + tokens, chans), BF16),
        pltpu.VMEM((2, tokens, chans), BF16),
        pltpu.VMEM((2, taps, chans), F32),
        *[pltpu.VMEM((length, length), BF16) for _ in range(4)],
        pltpu.VMEM((2, length, chans), F32),
        pltpu.VMEM((2, length, chans), F32),
        pltpu.VMEM((2, length, chans), F32),
        pltpu.VMEM((2, halo + tokens, chans), F32),
        pltpu.VMEM((2, tokens, chans), F32),
        pltpu.VMEM((2, tokens, chans), F32),
        pltpu.VMEM((length, chans), BF16),
        pltpu.VMEM((length, chans), BF16),
        pltpu.VMEM((2, length + 32, chans), F32),
        pltpu.VMEM((2, tokens + 32, chans), F32),
        pltpu.VMEM((2, tokens, chans), F32),
        pltpu.VMEM((2, halo, chans), BF16),
        pltpu.VMEM((2, halo, chans), BF16),
        pltpu.VMEM((1, halo + 16, chans), F32),
        pltpu.VMEM((2, taps, chans), F32),
        pltpu.VMEM((taps, chans), F32),
        pltpu.VMEM((2, 2 * EXTRA, chans // 2), F32),
        pltpu.VMEM((2 * EXTRA, chans // 2), F32),
        pltpu.VMEM((2 * EXTRA, chans // 2), F32),
        pltpu.VMEM((2 * EXTRA, chans // 2), F32),
        pltpu.VMEM((xs, slice_rows, chans), BF16),
        pltpu.VMEM((xs, slice_rows, chans), BF16),
        pltpu.VMEM((xs, 2 * EXTRA, chans // 2), BF16),
        pltpu.VMEM((ys, slice_rows, chans), F32),
        pltpu.VMEM((ys, 2 * EXTRA, chans // 2), F32),
        pltpu.VMEM((2 * xs, slice_rows, chans), BF16),
        pltpu.VMEM(gate_taps.shape, F32),
        pltpu.VMEM(value_featurizer_weights.shape, F32),
        pltpu.SemaphoreType.DMA((4,)),
        pltpu.SemaphoreType.DMA((4,)),
        pltpu.SemaphoreType.DMA((2,)),
        pltpu.SemaphoreType.DMA((2,)),
        pltpu.SemaphoreType.DMA((2,)),
        pltpu.SemaphoreType.DMA((2,)),
        pltpu.SemaphoreType.DMA((8,)),
        pltpu.SemaphoreType.DMA((8,)),
        pltpu.SemaphoreType.DMA((8,)),
    ]
    results = pl.pallas_call(
        functools.partial(kernel, (nctx, ntp, xs, ys, taps, scale)),
        out_shape=(
            jax.ShapeDtypeStruct((tokens, width), BF16),
            jax.ShapeDtypeStruct((taps, width), F32),
            jax.ShapeDtypeStruct(gate_taps.shape, F32),
            jax.ShapeDtypeStruct(value_featurizer_weights.shape, F32),
        ),
        in_specs=[hbm] * 9,
        out_specs=(vmem, vmem, vmem, vmem),
        scratch_shapes=scratch,
        compiler_params=pltpu.CompilerParams(
            collective_id=0, has_side_effects=True, vmem_limit_bytes=55_900_000
        ),
    )(
        out_grad, saved_input, explicit_filter_weights, gate_taps, value_featurizer_weights,
        *matrices,
    )
    return pl.pallas_call(
        write_out,
        out_shape=[jax.ShapeDtypeStruct(r.shape, r.dtype) for r in results],
        in_specs=[vmem] * 4,
        out_specs=[hbm] * 4,
        scratch_shapes=[pltpu.SemaphoreType.DMA((4,))],
        compiler_params=pltpu.CompilerParams(vmem_limit_bytes=2**20),
    )(*results)


def solution(mesh):
    placed = (
        P(("ctx", "tp"), None),
        P(("ctx", "tp"), None),
        P(None, "tp"),
        P(None, "tp"),
        P(None, "tp"),
    )
    return jax.shard_map(
        functools.partial(shards, mesh),
        mesh=mesh,
        in_specs=placed,
        out_specs=(P("ctx", "tp"), P(None, "tp"), P(None, "tp"), P(None, "tp")),
        check_vma=False,
    )
```

```python
import functools
import math

import jax
import jax.numpy as jnp
import ml_dtypes
import numpy as np
from jax import lax
from jax.experimental import pallas as pl
from jax.experimental.pallas import tpu as pltpu
from jax.sharding import PartitionSpec as P

MESH = pl.DeviceIdType.MESH
F32 = jnp.float32
BF16 = jnp.bfloat16
EXTRA = 8


def two_parts(matrix):
    high = matrix.astype(ml_dtypes.bfloat16)
    low = (matrix - high.astype(np.float64)).astype(ml_dtypes.bfloat16)
    return high, low


def transforms(length):
    odd = 2 * np.arange(length // 2)[:, None] + 1
    steps = (odd * np.arange(length)[None, :]) % (2 * length)
    angle = np.pi * steps / length
    forward = np.concatenate([np.cos(angle), -np.sin(angle)])
    inverse = forward.T * (2.0 / length)
    return two_parts(forward) + two_parts(inverse)


def split(x):
    high = x.astype(BF16)
    return high, (x - high.astype(F32)).astype(BF16)


def dot3(ah, al, xh, xl):
    def dot(a, b):
        return jnp.dot(a, b, preferred_element_type=F32)

    return dot(ah, xh) + dot(ah, xl) + dot(al, xh)


def kernel(
    sizes,
    og, si, h_hbm, gt_hbm, w_hbm, fh_hbm, fl_hbm, ih_hbm, il_hbm,
    ig_out, efg_out, gate_out, value_out,
    ubuf, gbuf, hb, fh, fl, ih, il,
    hs, vs, ds, uf, qb, zb, xh, xl, w1b, dqb, igb, head, head_in,
    uh, part, part_in, ep, ep_in, ext, ext_in, rs, xr, xe, yr, ye, ag, gt_ref, w_ref,
    a2a_send, a2a_recv, halo_send, halo_recv, head_send, head_recv,
    const_sem, one_send, one_recv,
):
    nctx, ntp, xs, ys, taps, scale = sizes
    rows, width = og.shape[0], og.shape[1] // ntp
    tokens = rows * ntp
    chans = width // 2
    halo = ubuf.shape[1] - tokens
    length = tokens + taps
    half_len = length // 2
    slice_rows = taps // xs
    ctx, tp = lax.axis_index("ctx"), lax.axis_index("tp")
    core = lax.rem(ctx, 2)
    x = lax.rem(ctx // 2, xs)
    ylo = ctx // (2 * xs)
    deep = ntp // 2
    tp_far = sorted(range(deep), key=lambda d: -min(d, deep - d))
    tp_order = [(far, d) for d in tp_far for far in (1, 0) if far or d]
    x_order = sorted(range(1, xs), key=lambda d: -min(d, xs - d))
    row_order = [(d, c) for d in x_order for c in range(2)] + [(0, 1)]

    def remote(src, dst, send, recv, to_ctx, to_tp):
        return pltpu.make_async_remote_copy(
            src_ref=src, dst_ref=dst, send_sem=send, recv_sem=recv,
            device_id=(to_ctx, to_tp), device_id_type=MESH,
        )

    def finish(ref, sem):
        pltpu.make_async_copy(ref, ref, sem).wait()

    def offset(k):
        half = (1 - core) if k == 0 else core
        return pl.multiple_of(half * chans, chans)

    def tp_peer(step):
        far, d = step
        return lax.rem(tp // deep + far, 2) * deep + lax.rem(lax.rem(tp, deep) + d, deep)

    def x_peer(d):
        return lax.rem(x + d, xs)

    def row_peer(step):
        d, c = step
        return (ylo * xs + x_peer(d)) * 2 + lax.rem(core + c, 2)

    def x_ctx(other):
        return (ylo * xs + other) * 2 + core

    def y_ctx(i):
        low = ylo < ys // 2
        pair = [jnp.where(low, ys - 1, 0), jnp.where(low, ys - 2, 1)]
        other = ylo + 1 - 2 * lax.rem(ylo, 2)
        to = [pair[0], pair[1], other][i - 1] if ys == 4 else lax.rem(ylo + i, ys)
        return (to * xs + x) * 2 + core

    barrier = pltpu.get_barrier_semaphore()

    def greet(to_ctx, to_tp):
        pl.semaphore_signal(barrier, inc=1, device_id=(to_ctx, to_tp), device_id_type=MESH)

    for step in tp_order:
        greet(ctx, tp_peer(step))
    for step in row_order:
        greet(row_peer(step), tp)
    for i in range(1, ys):
        greet(y_ctx(i), tp)

    @pl.when(ctx > 0)
    def _():
        greet(ctx - 1, tp)

    @pl.when(ctx < nctx - 1)
    def _():
        greet(ctx + 1, tp)

    constants = [
        pltpu.make_async_copy(src, dst, const_sem.at[i])
        for i, (src, dst) in enumerate(
            [(fh_hbm, fh), (fl_hbm, fl), (ih_hbm, ih), (il_hbm, il), (gt_hbm, gt_ref), (w_hbm, w_ref)]
            + [(h_hbm.at[:, pl.ds(offset(k), chans)], hb.at[k]) for k in range(2)]
        )
    ]
    for copy in constants:
        copy.start()

    @pl.when(ctx == 0)
    def _():
        ubuf[:, 0:halo, :] = jnp.zeros((2, halo, chans), BF16)

    @pl.when(ctx == nctx - 1)
    def _():
        head_in[...] = jnp.zeros(head_in.shape, BF16)

    greeted = ntp - 1 + 2 * xs - 1 + ys - 1
    greeted = greeted + jnp.where(ctx > 0, 1, 0) + jnp.where(ctx < nctx - 1, 1, 0)
    pl.semaphore_wait(barrier, greeted)

    def exchange(src, dst, base, k, sem):
        def columns(who):
            return src.at[:, pl.ds(pl.multiple_of(who * width + offset(k), chans), chans)]

        place = dst.at[k, pl.ds(pl.multiple_of(base + tp * rows, 16), rows), :]
        for step in tp_order:
            to = tp_peer(step)
            remote(columns(to), place, a2a_send.at[sem], a2a_recv.at[sem], ctx, to).start()
        pltpu.make_async_copy(columns(tp), place, a2a_recv.at[sem]).start()

    exchange(si, ubuf, halo, 0, 0)
    exchange(si, ubuf, halo, 1, 1)
    exchange(og, gbuf, 0, 0, 2)
    exchange(og, gbuf, 0, 1, 3)

    for copy in constants:
        copy.wait()
    for k in range(2):
        th, tl = split(hb[k])
        hs[k] = dot3(fh[:, 0:taps], fl[:, 0:taps], th, tl)
    w1b[:, 0:16, :] = jnp.zeros((2, 16, chans), F32)
    w1b[:, 16 + length : 32 + length, :] = jnp.zeros((2, 16, chans), F32)
    dqb[:, 0:16, :] = jnp.zeros((2, 16, chans), F32)
    dqb[:, 16 + tokens : 32 + tokens, :] = jnp.zeros((2, 16, chans), F32)

    def taps_of(ref, k):
        block = ref[:, pl.ds(offset(k), chans)]
        return [block[i : i + 1] for i in range(3)]

    def halo_copy(k):
        return remote(
            ubuf.at[k, pl.ds(tokens, halo), :], ubuf.at[1 - k, pl.ds(0, halo), :],
            halo_send.at[k], halo_recv.at[1 - k], ctx + 1, tp,
        )

    def spectrum_product(a, a_k, b, b_k, sign):
        for r in range(0, half_len, 32):
            ar, ai = a[a_k, r : r + 32], a[a_k, half_len + r : half_len + r + 32]
            br, bi = b[b_k, r : r + 32], b[b_k, half_len + r : half_len + r + 32]
            if sign > 0:
                re, im = ar * br - ai * bi, ar * bi + ai * br
            else:
                re, im = ar * br + ai * bi, ar * bi - ai * br
            xh[r : r + 32], xl[r : r + 32] = split(re)
            xh[half_len + r : half_len + r + 32], xl[half_len + r : half_len + r + 32] = split(im)

    def delayed(ref, k, r, count):
        first = halo - taps + r
        return [ref[k, first - i : first - i + count] for i in range(3)]

    def mixed(weights, signals):
        return weights[0] * signals[0] + weights[1] * signals[1] + weights[2] * signals[2]

    def own_spectrum(k):
        finish(ubuf.at[k, pl.ds(halo, tokens), :], a2a_recv.at[k])

        @pl.when(ctx < nctx - 1)
        def _():
            halo_copy(k).start()

        wv, wg = taps_of(w_ref, k), taps_of(gt_ref, k)
        for r in range(halo, halo + tokens, 32):
            uf[k, r : r + 32] = ubuf[k, r : r + 32].astype(F32)
        for r in range(taps, length, 32):
            u = delayed(uf, k, r, 32)
            xh[r : r + 32], xl[r : r + 32] = split(mixed(wv, u))
            qb[k, r - taps : r - taps + 32] = mixed(wg, u)
        vs[k] = dot3(fh[:, taps:], fl[:, taps:], xh[taps:, :], xl[taps:, :])

    def halo_spectrum(k):
        @pl.when(ctx > 0)
        def _():
            finish(ubuf.at[k, pl.ds(0, halo), :], halo_recv.at[k])

        wv, wg = taps_of(w_ref, k), taps_of(gt_ref, k)
        for r in range(0, halo, 16):
            block = ubuf[k, r : r + 16].astype(F32)
            uf[k, r : r + 16] = block
            uh[0, r : r + 16] = block
        for r in range(0, taps + 16, 16):
            xh[r : r + 16], xl[r : r + 16] = split(mixed(wv, delayed(uh, 0, r, 16)))
        blank = jnp.zeros((tokens - taps - 16, chans), BF16)
        xh[taps + 16 : tokens] = blank
        xl[taps + 16 : tokens] = blank
        qb[k, 0:16] = mixed(wg, delayed(uf, k, taps, 16))
        vs[k] += dot3(fh[:, :tokens], fl[:, :tokens], xh[:tokens, :], xl[:tokens, :])
        spectrum_product(hs, k, vs, k, 1)
        zb[k] = dot3(ih[taps:, :], il[taps:, :], xh[...], xl[...])

    def fold(values):
        return jnp.sum(values.reshape(values.shape[0] // 8, 8, chans), axis=0)

    def input_gradient(k):
        wv, wg = taps_of(w_ref, k), taps_of(gt_ref, k)
        for r in range(0, halo + tokens, 16):
            a = [w1b[k, r + i : r + i + 16] for i in range(3)]
            total = wv[0] * a[0] + wv[1] * a[1] + wv[2] * a[2]
            first = r - halo
            if first >= -16:
                d = [dqb[k, 16 + first + i : 32 + first + i] for i in range(3)]
                total = total + wg[0] * d[0] + wg[1] * d[1] + wg[2] * d[2]
            if first < 0:
                head[k, r : r + 16] = total.astype(BF16)
            else:
                igb[k, first : first + 16] = total

        @pl.when(ctx > 0)
        def _():
            remote(
                head.at[k], head_in.at[1 - k], head_send.at[k], head_recv.at[1 - k], ctx - 1, tp
            ).start()

    partner = ctx + 1 - 2 * core

    def filter_part(k):
        finish(gbuf.at[k], a2a_recv.at[2 + k])
        for r in range(0, tokens, 32):
            g = gbuf[k, r : r + 32].astype(F32)
            xh[taps + r : taps + r + 32], xl[taps + r : taps + r + 32] = split(
                g * qb[k, r : r + 32]
            )
            dqb[k, 16 + r : 48 + r] = g * zb[k, r : r + 32]
        ds[k] = dot3(fh[:, taps:], fl[:, taps:], xh[taps:, :], xl[taps:, :])
        spectrum_product(vs, k, ds, k, -1)
        part[k] = dot3(ih[0:taps, :], il[0:taps, :], xh[...], xl[...]) * scale

    def extra_part(k):
        spectrum_product(hs, k, ds, k, -1)
        w1b[k, 16 : 16 + length] = dot3(ih[...], il[...], xh[...], xl[...])
        sums = [jnp.zeros((8, chans), F32) for _ in range(6)]
        for r in range(0, length, 32):
            u = delayed(uf, k, r, 32)
            w1 = w1b[k, 16 + r : 48 + r]
            if r >= taps:
                dq = dqb[k, 16 + r - taps : 48 + r - taps]
                sums[:3] = [s + fold(dq * d) for s, d in zip(sums[:3], u)]
            sums[3:] = [s + fold(w1 * d) for s, d in zip(sums[3:], u)]
        for i, s in enumerate(sums):
            total = jnp.sum(s, axis=0, keepdims=True) * scale
            for lane in range(2):
                ep[k, 8 * lane + i : 8 * lane + i + 1] = total[
                    :, lane * (chans // 2) : (lane + 1) * (chans // 2)
                ]

    ep[...] = jnp.zeros(ep.shape, F32)
    uf[:, halo - 16 : halo] = jnp.zeros((2, 16, chans), F32)
    uh[0, halo : halo + 16] = jnp.zeros((16, chans), F32)
    own_spectrum(0)
    own_spectrum(1)
    halo_spectrum(0)
    filter_part(0)
    remote(part.at[0], part_in, one_send.at[0], one_recv.at[0], partner, tp).start()
    halo_spectrum(1)
    extra_part(0)
    remote(ep.at[0], ep_in, one_send.at[7], one_recv.at[7], partner, tp).start()
    filter_part(1)
    finish(part_in, one_recv.at[0])
    for s in range(xs):
        rows_of = slice(s * slice_rows, (s + 1) * slice_rows)
        rs[s] = (part[1, rows_of] + part_in[rows_of]).astype(BF16)
    for d in x_order:
        to = x_peer(d)
        remote(rs.at[to], xr.at[x], one_send.at[1], one_recv.at[1], x_ctx(to), tp).start()
    xr[x] = rs[x]
    extra_part(1)
    finish(ep_in, one_recv.at[7])
    xe[x] = (ep[1] + ep_in[...]).astype(BF16)
    for d in x_order:
        remote(
            xe.at[x], xe.at[x], one_send.at[4], one_recv.at[4], x_ctx(x_peer(d)), tp
        ).start()
    input_gradient(0)
    input_gradient(1)
    finish(xr.at[pl.ds(0, xs - 1)], one_recv.at[1])
    total = xr[0].astype(F32)
    for s in range(1, xs):
        total = total + xr[s].astype(F32)
    yr[ylo] = total
    for i in range(1, ys):
        remote(
            yr.at[ylo], yr.at[ylo], one_send.at[2], one_recv.at[2], y_ctx(i), tp
        ).start()
    finish(xe.at[pl.ds(0, xs - 1)], one_recv.at[4])
    total = xe[0].astype(F32)
    for s in range(1, xs):
        total = total + xe[s].astype(F32)
    ye[ylo] = total
    for i in range(1, ys):
        remote(
            ye.at[ylo], ye.at[ylo], one_send.at[5], one_recv.at[5], y_ctx(i), tp
        ).start()

    @pl.when(ctx < nctx - 1)
    def _():
        for k in range(2):
            finish(head_in.at[k], head_recv.at[k])

    for k in range(2):
        for r in range(0, tokens, 16):
            block = igb[k, r : r + 16]
            late = r - (tokens - halo)
            if late >= 0:
                block = block + head_in[k, late : late + 16].astype(F32)
            ig_out[r : r + 16, pl.ds(offset(k), chans)] = block.astype(BF16)

    finish(yr.at[pl.ds(0, ys - 1)], one_recv.at[2])
    total = yr[0]
    for s in range(1, ys):
        total = total + yr[s]
    slot = core * xs + x
    ag[slot] = total.astype(BF16)
    for step in row_order:
        remote(
            ag.at[slot], ag.at[slot], one_send.at[3], one_recv.at[3], row_peer(step), tp
        ).start()
    finish(ye.at[pl.ds(0, ys - 1)], one_recv.at[5])
    total = ye[0]
    for s in range(1, ys):
        total = total + ye[s]
    ext[...] = total
    remote(ext, ext_in, one_send.at[6], one_recv.at[6], partner, tp).start()

    def put_extra(source, k):
        for lane in range(2):
            place = pl.ds(pl.multiple_of(offset(k) + lane * (chans // 2), chans // 2), chans // 2)
            gate_out[:, place] = source[8 * lane : 8 * lane + 3]
            value_out[:, place] = source[8 * lane + 3 : 8 * lane + 6]

    put_extra(ext, 1)
    finish(ext_in, one_recv.at[6])
    put_extra(ext_in, 0)
    for k in range(2):
        finish(ubuf.at[k, pl.ds(0, rows * (ntp - 1)), :], a2a_send.at[k])
        finish(gbuf.at[k, pl.ds(0, rows * (ntp - 1)), :], a2a_send.at[2 + k])

        @pl.when(ctx < nctx - 1)
        def _(k=k):
            finish(ubuf.at[k, pl.ds(0, halo), :], halo_send.at[k])

        @pl.when(ctx > 0)
        def _(k=k):
            finish(head.at[k], head_send.at[k])

    finish(rs.at[pl.ds(0, xs - 1)], one_send.at[1])
    finish(yr.at[pl.ds(0, ys - 1)], one_send.at[2])
    finish(xe.at[pl.ds(0, xs - 1)], one_send.at[4])
    finish(ye.at[pl.ds(0, ys - 1)], one_send.at[5])
    finish(ext, one_send.at[6])
    finish(part_in, one_send.at[0])
    finish(ep_in, one_send.at[7])

    finish(ag.at[pl.ds(0, 2 * xs - 1)], one_recv.at[3])
    for half in range(2):
        for s in range(xs):
            efg_out[
                s * slice_rows : (s + 1) * slice_rows, half * chans : (half + 1) * chans
            ] = ag[half * xs + s].astype(F32)
    finish(ag.at[pl.ds(0, 2 * xs - 1)], one_send.at[3])


def write_out(*refs):
    copies = [
        pltpu.make_async_copy(refs[i], refs[4 + i], refs[8].at[i]) for i in range(4)
    ]
    for copy in copies:
        copy.start()
    for copy in copies:
        copy.wait()


def shards(mesh, out_grad, saved_input, explicit_filter_weights, gate_taps, value_featurizer_weights):
    nctx, ntp = mesh.shape["ctx"], mesh.shape["tp"]
    rows, channels = out_grad.shape
    width = channels // ntp
    tokens = rows * ntp
    taps = explicit_filter_weights.shape[0]
    xs = 8 if nctx >= 64 else 2
    ys = nctx // (2 * xs)
    chans = width // 2
    halo = -(-(taps + gate_taps.shape[0] - 2) // 16) * 16
    length = tokens + taps
    slice_rows = taps // xs
    scale = np.float32(1.0 / math.sqrt(tokens * nctx))
    matrices = [jnp.asarray(m) for m in transforms(length)]
    hbm = pl.BlockSpec(memory_space=pltpu.HBM)
    vmem = pl.BlockSpec(memory_space=pltpu.VMEM)
    gate_taps = pltpu.with_memory_space_constraint(gate_taps, pltpu.HBM)
    value_featurizer_weights = pltpu.with_memory_space_constraint(value_featurizer_weights, pltpu.HBM)
    scratch = [
        pltpu.VMEM((2, halo + tokens, chans), BF16),
        pltpu.VMEM((2, tokens, chans), BF16),
        pltpu.VMEM((2, taps, chans), F32),
        *[pltpu.VMEM((length, length), BF16) for _ in range(4)],
        pltpu.VMEM((2, length, chans), F32),
        pltpu.VMEM((2, length, chans), F32),
        pltpu.VMEM((2, length, chans), F32),
        pltpu.VMEM((2, halo + tokens, chans), F32),
        pltpu.VMEM((2, tokens, chans), F32),
        pltpu.VMEM((2, tokens, chans), F32),
        pltpu.VMEM((length, chans), BF16),
        pltpu.VMEM((length, chans), BF16),
        pltpu.VMEM((2, length + 32, chans), F32),
        pltpu.VMEM((2, tokens + 32, chans), F32),
        pltpu.VMEM((2, tokens, chans), F32),
        pltpu.VMEM((2, halo, chans), BF16),
        pltpu.VMEM((2, halo, chans), BF16),
        pltpu.VMEM((1, halo + 16, chans), F32),
        pltpu.VMEM((2, taps, chans), F32),
        pltpu.VMEM((taps, chans), F32),
        pltpu.VMEM((2, 2 * EXTRA, chans // 2), F32),
        pltpu.VMEM((2 * EXTRA, chans // 2), F32),
        pltpu.VMEM((2 * EXTRA, chans // 2), F32),
        pltpu.VMEM((2 * EXTRA, chans // 2), F32),
        pltpu.VMEM((xs, slice_rows, chans), BF16),
        pltpu.VMEM((xs, slice_rows, chans), BF16),
        pltpu.VMEM((xs, 2 * EXTRA, chans // 2), BF16),
        pltpu.VMEM((ys, slice_rows, chans), F32),
        pltpu.VMEM((ys, 2 * EXTRA, chans // 2), F32),
        pltpu.VMEM((2 * xs, slice_rows, chans), BF16),
        pltpu.VMEM(gate_taps.shape, F32),
        pltpu.VMEM(value_featurizer_weights.shape, F32),
        pltpu.SemaphoreType.DMA((4,)),
        pltpu.SemaphoreType.DMA((4,)),
        pltpu.SemaphoreType.DMA((2,)),
        pltpu.SemaphoreType.DMA((2,)),
        pltpu.SemaphoreType.DMA((2,)),
        pltpu.SemaphoreType.DMA((2,)),
        pltpu.SemaphoreType.DMA((8,)),
        pltpu.SemaphoreType.DMA((8,)),
        pltpu.SemaphoreType.DMA((8,)),
    ]
    results = pl.pallas_call(
        functools.partial(kernel, (nctx, ntp, xs, ys, taps, scale)),
        out_shape=(
            jax.ShapeDtypeStruct((tokens, width), BF16),
            jax.ShapeDtypeStruct((taps, width), F32),
            jax.ShapeDtypeStruct(gate_taps.shape, F32),
            jax.ShapeDtypeStruct(value_featurizer_weights.shape, F32),
        ),
        in_specs=[hbm] * 9,
        out_specs=(vmem, vmem, vmem, vmem),
        scratch_shapes=scratch,
        compiler_params=pltpu.CompilerParams(
            collective_id=0, has_side_effects=True, vmem_limit_bytes=55_900_000
        ),
    )(
        out_grad, saved_input, explicit_filter_weights, gate_taps, value_featurizer_weights,
        *matrices,
    )
    return pl.pallas_call(
        write_out,
        out_shape=[jax.ShapeDtypeStruct(r.shape, r.dtype) for r in results],
        in_specs=[vmem] * 4,
        out_specs=[hbm] * 4,
        scratch_shapes=[pltpu.SemaphoreType.DMA((4,))],
        compiler_params=pltpu.CompilerParams(vmem_limit_bytes=2**20),
    )(*results)


def solution(mesh):
    placed = (
        P(("ctx", "tp"), None),
        P(("ctx", "tp"), None),
        P(None, "tp"),
        P(None, "tp"),
        P(None, "tp"),
    )
    return jax.shard_map(
        functools.partial(shards, mesh),
        mesh=mesh,
        in_specs=placed,
        out_specs=(P("ctx", "tp"), P(None, "tp"), P(None, "tp"), P(None, "tp")),
        check_vma=False,
    )
```
